32 devices in a mesh: ia: 4 (over x, core), ja: 8 (over z, y).
Axes of the slice: x: 2, y: 2, z: 4, core: 2. Of those that a mesh axis runs over, the one named last changes fastest.
Arguments:
- star_pos: float32 [3, 32768], P(None, ('ia', 'ja')), may hold values from -6 to 6
- star_vel: float32 [3, 32768], P(None, ('ia', 'ja')), may hold values from -3 to 3
- star_acc: float32 [3, 32768], P(None, ('ia', 'ja')), may hold values from -3 to 3
- star_jerk: float32 [3, 32768], P(None, ('ia', 'ja')), may hold values from -6 to 6
- star_mass: float32 [32768], P(('ia', 'ja')), may hold values from 6.1035157e-06 to 0.00015258789
- star_level: int32 [32768], P(('ia', 'ja')), may hold values from 0 to 5, as said below
- active_index: int32 [256], P(('ia', 'ja')), may hold values from 0 to 1023, as said below
- active_count: int32 [32], P(('ia', 'ja')), may hold values from 1 to 8, as said below
Outputs:
- updated: float32 [12, 256], P(None, ('ia', 'ja'))
The draws below stay inside these ranges and needn't reach their ends.
Inputs may be any that keep to these rules, and one draw needn't show every extreme that they name: active_count[b] is the number of active stars of owner block b; some block has exactly 8, not always the same one. `active_index`: the slots of owner block b hold distinct local star numbers of that block; the first active_count[b] of them are exactly the stars of the block with star_level 3 or more, the others name inactive stars of the block. `star_level`: A star is active at this step exactly when its level is 3 or more.
All inputs are finite; a program needn't handle non-finite values.
Results may differ from the reference program's by a relative error of at most 0.0003.
Values sent between devices are 32-bit elements; how exact they have to be, the bound alone decides.
A program may use at most 64 MiB of HBM per device.

```python
import math
import jax
import jax.numpy as jnp
from jax import lax

STAR_DEV = 1024
ACT_CAP = 8
OWNERS = 32
NSTARS = 32768
SLOTS = 256


def active_plan(key):
    plan_key = jax.random.fold_in(key, 4711)
    count_key, order_key, full_key, slow_key, fast_key = jax.random.split(plan_key, 5)
    counts = jax.random.randint(count_key, (OWNERS,), 1, ACT_CAP + 1)
    fullest = jax.random.randint(full_key, (), 0, OWNERS)
    counts = counts.at[fullest].set(ACT_CAP)
    owner_keys = jax.random.split(order_key, OWNERS)
    orders = jax.vmap(lambda owner_key: jax.random.permutation(owner_key, STAR_DEV))(owner_keys)
    chosen = orders[:, :ACT_CAP].astype(jnp.int32)
    live_flags = (jnp.arange(ACT_CAP)[None, :] < counts[:, None]).astype(jnp.int32)
    owner_rows = jnp.broadcast_to(jnp.arange(OWNERS)[:, None], (OWNERS, ACT_CAP))
    flags = jnp.zeros((OWNERS, STAR_DEV), jnp.int32).at[owner_rows, chosen].set(live_flags)
    slow_levels = jax.random.randint(slow_key, (OWNERS, STAR_DEV), 0, 3)
    fast_levels = jax.random.randint(fast_key, (OWNERS, STAR_DEV), 3, 6)
    levels = jnp.where(flags == 1, fast_levels, slow_levels)
    return (chosen.reshape(-1), counts.astype(jnp.int32), levels.reshape(-1).astype(jnp.int32))


def draw_active_index(key, part):
    return active_plan(key)[0]


def draw_active_count(key, part):
    return active_plan(key)[1]


def draw_star_level(key, part):
    return active_plan(key)[2]


def level_of(own_key, extent, cuts, low, high):
    gain = 1.0
    for position, shards_of in cuts:
        heights = jax.random.uniform(jax.random.fold_in(jax.random.fold_in(own_key, 6), position), (shards_of,), jnp.float32, low / len(cuts), high / len(cuts))
        gain = gain * jnp.repeat(jnp.exp(heights), extent[position] // shards_of).reshape((-1,) + (1,) * (len(extent) - 1 - position))
    return gain


def normal_values(key, dims, spread, most, cuts=(), held_as=jnp.bfloat16):
    result = jax.random.normal(key, dims, jnp.float32) * spread
    if len(cuts) > 0:
        result = level_of(key, dims, cuts, -0.22, 0.18) * result
    return jnp.clip(result, min=-most, max=most).astype(held_as)


def setup_inputs(seed: int = 0) -> dict:
    arg_keys = jax.random.split(jax.random.key(seed), 9)
    return {
        "star_pos": normal_values(arg_keys[0], (3, NSTARS), 1.0, 6.0, ((1, 32),), jnp.float32),
        "star_vel": normal_values(arg_keys[1], (3, NSTARS), 0.5, 3.0, ((1, 32),), jnp.float32),
        "star_acc": normal_values(arg_keys[2], (3, NSTARS), 0.5, 3.0, ((1, 32),), jnp.float32),
        "star_jerk": normal_values(arg_keys[3], (3, NSTARS), 1.0, 6.0, ((1, 32),), jnp.float32),
        "star_mass": jnp.clip(jnp.exp(math.log(0.00015258789) - 3.218876 * jax.random.uniform(arg_keys[4], (NSTARS,), jnp.float32) ** level_of(arg_keys[4], (NSTARS,), ((0, 32),), -0.2, 0.2)), 6.10351571594947e-06, 0.00015258789),
        "star_level": draw_star_level(jax.random.fold_in(arg_keys[8], 71), 0),
        "active_index": draw_active_index(jax.random.fold_in(arg_keys[8], 71), 0),
        "active_count": draw_active_count(jax.random.fold_in(arg_keys[8], 71), 0),
    }


tick_now = 44
top_level = 5
tick_length = 0.125
soft_square = 0.0001

def star_age(levels):
    periods = jnp.left_shift(jnp.ones_like(levels), top_level - levels)
    remains = jnp.remainder(jnp.full_like(levels, tick_now), periods)
    ticks = jnp.where(remains == 0, periods, remains)
    return ticks.astype(jnp.float32) * tick_length

def predict(positions, velocity, accelerations, jerk_rates, star_ages):
    elapsed = star_ages[None, :]
    new_pos = positions + elapsed * (velocity + elapsed * (accelerations * 0.5 + elapsed * jerk_rates / 6.0))
    new_vel = velocity + elapsed * (accelerations + elapsed * jerk_rates * 0.5)
    return (new_pos, new_vel)

def pair_block(targets, sources):
    delta_pos = [sources[axis_num][None, :] - targets[axis_num][:, None] for axis_num in range(3)]
    delta_vel = [sources[3 + axis_num][None, :] - targets[3 + axis_num][:, None] for axis_num in range(3)]
    squared = delta_pos[0] * delta_pos[0] + delta_pos[1] * delta_pos[1] + delta_pos[2] * delta_pos[2] + soft_square
    inverse = lax.rsqrt(squared)
    inverse_sq = inverse * inverse
    strength = sources[6][None, :] * inverse * inverse_sq
    radial = 3.0 * (delta_pos[0] * delta_vel[0] + delta_pos[1] * delta_vel[1] + delta_pos[2] * delta_vel[2]) * inverse_sq
    results = [lax.optimization_barrier(jnp.sum(strength * delta_pos[axis_num], axis=1)) for axis_num in range(3)]
    results = results + [lax.optimization_barrier(jnp.sum(strength * (delta_vel[axis_num] - radial * delta_pos[axis_num]), axis=1)) for axis_num in range(3)]
    return jnp.stack(results)

def correct(targets, forces, old_acc, old_jerk, step_sizes, live_mask):
    new_acc = forces[:3]
    new_jerk = forces[3:]
    elapsed = step_sizes[None, :]
    change = old_acc - new_acc
    snap_part = -6.0 * change - elapsed * (4.0 * old_jerk + 2.0 * new_jerk)
    crackle_part = 12.0 * change + 6.0 * elapsed * (old_jerk + new_jerk)
    cor_pos = targets[:3] + elapsed * elapsed * (snap_part / 24.0 + crackle_part / 120.0)
    cor_vel = targets[3:] + elapsed * (snap_part / 6.0 + crackle_part / 24.0)
    stacked = jnp.concatenate([cor_pos, cor_vel, new_acc, new_jerk], 0)
    return jnp.where(live_mask[None, :], stacked, 0.0)

def reference(star_pos, star_vel, star_acc, star_jerk, star_mass, star_level, active_index, active_count):
    star_ages = star_age(star_level)
    pred_pos, pred_vel = predict(star_pos, star_vel, star_acc, star_jerk, star_ages)
    slot_ids = jnp.arange(SLOTS, dtype=jnp.int32)
    owner_ids = slot_ids // ACT_CAP
    chosen = (owner_ids * STAR_DEV + active_index).astype(jnp.int32)
    live_mask = slot_ids % ACT_CAP < active_count[owner_ids]
    targets = jnp.concatenate([pred_pos[:, chosen], pred_vel[:, chosen]], 0)
    sources = jnp.concatenate([pred_pos, pred_vel, star_mass[None, :]], 0)
    tile_rows = math.gcd(SLOTS, 64)
    tile_cols = math.gcd(NSTARS, 8192)
    tiles = jnp.transpose(targets.reshape(6, SLOTS // tile_rows, tile_rows), (1, 0, 2))
    source_blocks = jnp.transpose(sources.reshape(7, NSTARS // tile_cols, tile_cols), (1, 0, 2))

    def one_tile(target_tile):

        def advance(running, source_part):
            return (running + pair_block(target_tile, source_part), None)
        totals, unused = lax.scan(advance, jnp.zeros((6, tile_rows), jnp.float32), source_blocks)
        return totals
    forces = jnp.transpose(lax.map(one_tile, tiles), (1, 0, 2)).reshape(6, SLOTS)
    return correct(targets, forces, star_acc[:, chosen], star_jerk[:, chosen], star_ages[chosen], live_mask)
```

```python
import functools

import jax
import jax.numpy as jnp
from jax import lax
from jax.experimental import pallas as pl
from jax.experimental.pallas import tpu as pltpu
from jax.sharding import PartitionSpec as P

tick_now = 44
top_level = 5
tick_length = 0.125
soft_square = 0.0001
first_active_level = 3

LANES = 128
SOURCE_PARTS = 4
FAR = 64


def kernel(
    shape, pos_hbm, vel_hbm, acc_hbm, jerk_hbm, mass_hbm, level_hbm, idx_hbm, out_ref,
    pos, vel, acc, jerk, mass, level, idx, src, tgt, wide, sums, part, got,
    in_sem, src_send, src_recv, tgt_send, tgt_recv, red_send, red_recv, ready,
):
    n_ia, n_ja, s = shape
    n_lo = n_ja // s
    t = n_ia * n_lo
    flip = 1 if n_ia % 2 == 0 else 0
    stars = pos.shape[1]
    cap = idx.shape[0]
    ia, ja = lax.axis_index("ia"), lax.axis_index("ja")
    hi, lo = ja // n_lo, ja % n_lo
    me = lo * n_ia + ia
    mesh_id = pl.DeviceIdType.MESH

    def mate(p):
        return (p % n_ia, hi * n_lo + p // n_ia)

    def partner(o):
        other = ia + 1 - 2 * (ia % 2) if flip else ia
        return (other, o * n_lo + lo)

    def nearest(o):
        up = o + jnp.where(o >= hi, 1, 0)
        down = s - 1 - o - jnp.where(o >= s - 1 - hi, 1, 0)
        return jnp.where(2 * hi < s, up, down)

    def src_copy(o):
        return pltpu.make_async_remote_copy(
            src_ref=src.at[hi], dst_ref=src.at[hi], send_sem=src_send.at[o],
            recv_sem=src_recv.at[hi], device_id=partner(o), device_id_type=mesh_id)

    def src_arrival(o):
        return pltpu.make_async_remote_copy(
            src_ref=src.at[o], dst_ref=src.at[o], send_sem=src_send.at[o],
            recv_sem=src_recv.at[o], device_id=partner(o), device_id_type=mesh_id)

    def tgt_copy(p):
        return pltpu.make_async_remote_copy(
            src_ref=tgt.at[me], dst_ref=tgt.at[me], send_sem=tgt_send.at[p],
            recv_sem=tgt_recv.at[me], device_id=mate(p), device_id_type=mesh_id)

    def tgt_arrival(p):
        return pltpu.make_async_remote_copy(
            src_ref=tgt.at[p], dst_ref=tgt.at[p], send_sem=tgt_send.at[p],
            recv_sem=tgt_recv.at[p], device_id=mate(p), device_id_type=mesh_id)

    def red_copy(p):
        return pltpu.make_async_remote_copy(
            src_ref=part.at[p], dst_ref=got.at[me], send_sem=red_send.at[p],
            recv_sem=red_recv.at[me], device_id=mate(p), device_id_type=mesh_id)

    def red_arrival(p):
        return pltpu.make_async_remote_copy(
            src_ref=got.at[p], dst_ref=got.at[p], send_sem=red_send.at[p],
            recv_sem=red_recv.at[p], device_id=mate(p), device_id_type=mesh_id)

    def each(low, high, body):
        def step(k, carry):
            body(k)
            return carry
        lax.fori_loop(low, high, step, 0)

    def others(body):
        def step(p):
            @pl.when(p != me)
            def other():
                body(p)
        each(0, t, step)

    barrier = pltpu.get_barrier_semaphore()

    def greet(device):
        pl.semaphore_signal(barrier, inc=1, device_id=device, device_id_type=mesh_id)

    loads = [
        pltpu.make_async_copy(a, b, in_sem.at[i])
        for i, (a, b) in enumerate(
            [(level_hbm, level), (pos_hbm, pos), (vel_hbm, vel), (acc_hbm, acc),
             (jerk_hbm, jerk), (mass_hbm, mass), (idx_hbm, idx)])
    ]
    for load in loads:
        load.start()
    each(hi + 1, s, lambda o: greet(partner(o)))
    others(lambda p: greet(mate(p)))
    for load in loads[:6]:
        load.wait()

    periods = jnp.left_shift(jnp.ones((1, stars), jnp.int32), top_level - level[...])
    remains = jnp.bitwise_and(tick_now, periods - 1)
    age = jnp.where(remains == 0, periods, remains).astype(jnp.float32) * tick_length
    pred_pos = pos[...] + age * (
        vel[...] + age * (acc[...] * 0.5 + age * jerk[...] * (1.0 / 6.0)))
    pred_vel = vel[...] + age * (acc[...] + age * jerk[...] * 0.5)
    src[hi, 0:3] = pred_pos
    src[hi, 3:6] = pred_vel
    src[hi, 6:7] = mass[...]
    src[hi, 7:8] = age

    pl.semaphore_wait(barrier, t - 1 + hi)
    each(0, hi, lambda o: src_copy(o).start())

    def tell(o):
        pl.semaphore_signal(ready.at[hi], inc=1, device_id=partner(o), device_id_type=mesh_id)

    each(0, hi, tell)

    loads[6].wait()
    slot = lax.broadcasted_iota(jnp.int32, (cap, stars), 0)
    want = jnp.zeros((cap, stars), jnp.int32)
    for i in range(cap):
        want = jnp.where(slot == i, idx[i], want)
    mask = lax.broadcasted_iota(jnp.int32, (cap, stars), 1) == want

    def pick(row):
        return jnp.sum(jnp.where(mask, row, 0.0), axis=1, keepdims=True)

    lane = lax.broadcasted_iota(jnp.int32, (cap, LANES), 1)

    def columns(values):
        tile = jnp.zeros((cap, LANES), jnp.float32)
        for i, value in values:
            tile = jnp.where(lane == i, value, tile)
        return tile

    own = [pick(src[hi, q:q + 1]) for q in range(6)]
    tgt[me] = columns(enumerate(own))
    others(lambda p: tgt_copy(p).start())

    old_acc = [pick(acc[q:q + 1, :]) for q in range(3)]
    old_jerk = [pick(jerk[q:q + 1, :]) for q in range(3)]
    h = pick(src[hi, 7:8])
    live = pick(level[...].astype(jnp.float32)) > first_active_level - 0.5
    h2 = h * h
    fixed = [own[q] - h2 * (0.15 * old_acc[q] + (7.0 / 60.0) * h * old_jerk[q])
             for q in range(3)]
    fixed += [own[3 + q] - h * (0.5 * old_acc[q] + (5.0 / 12.0) * h * old_jerk[q])
              for q in range(3)]
    constant = columns(enumerate(fixed))
    factor = columns([(q, 0.15 * h2) for q in range(3)] + [(3 + q, 0.5 * h) for q in range(3)]
                     + [(6 + q, 1.0) for q in range(6)]
                     + [(FAR + q, h2 * h * (-1.0 / 30.0)) for q in range(3)]
                     + [(FAR + 3 + q, h2 * (-1.0 / 12.0)) for q in range(3)])

    def pairs(target, j, totals):
        totals = list(totals)
        for c in range(stars // LANES):
            row = [src[j, q:q + 1, c * LANES:(c + 1) * LANES] for q in range(7)]
            d = [row[q] - target[q] for q in range(3)]
            w = [row[3 + q] - target[3 + q] for q in range(3)]
            u = lax.rsqrt(d[0] * d[0] + d[1] * d[1] + d[2] * d[2] + soft_square)
            u2 = u * u
            m = row[6] * u * u2
            r = 3.0 * (d[0] * w[0] + d[1] * w[1] + d[2] * w[2]) * u2
            for q in range(3):
                totals[q] = totals[q] + m * d[q]
                totals[3 + q] = totals[3 + q] + m * (w[q] - r * d[q])
        return totals

    def first(p):
        tile = tgt[p]
        target = [jnp.broadcast_to(tile[:, q:q + 1], (cap, LANES)) for q in range(6)]
        total = pairs(target, hi, [jnp.zeros((cap, LANES), jnp.float32)] * 6)
        for q in range(6):
            wide[p, q] = target[q]
            sums[p, q] = total[q]

    def middle(p, j):
        total = pairs([wide[p, q] for q in range(6)], j, [sums[p, q] for q in range(6)])
        for q in range(6):
            sums[p, q] = total[q]

    def last(p, j):
        total = pairs([wide[p, q] for q in range(6)], j, [sums[p, q] for q in range(6)])
        force = [jnp.sum(x, axis=1, keepdims=True) for x in total]
        part[p] = columns([(i, force[i % 3]) for i in range(9)]
                          + [(9 + q, force[3 + q]) for q in range(3)]
                          + [(FAR + i, force[3 + i % 3]) for i in range(6)])

        @pl.when(p != me)
        def send():
            red_copy(p).start()

    def reply(o):
        pl.semaphore_wait(ready.at[o], 1)
        src_copy(o).start()

    each(hi + 1, jnp.minimum(hi + 3, s), reply)
    others(lambda p: tgt_arrival(p).wait_recv())
    each(0, t, first)
    each(jnp.minimum(hi + 3, s), s, reply)

    def block(o):
        j = nearest(o)
        src_arrival(j).wait_recv()
        each(0, t, lambda p: middle(p, j))

    each(0, s - 2, block)
    end = nearest(s - 2)
    src_arrival(end).wait_recv()
    each(0, t, lambda p: last(p, end))
    got[me] = part[me]

    def collect(p, total):
        @pl.when(p != me)
        def other():
            red_arrival(p).wait_recv()
        return total + got[p]

    total = lax.fori_loop(0, t, collect, jnp.zeros((cap, LANES), jnp.float32)) * factor
    result = constant + total + pltpu.roll(total, LANES - FAR, 1)
    out_ref[...] = jnp.where(live, result, 0.0)[:, :12]

    def drain(p):
        tgt_copy(p).wait_send()
        red_copy(p).wait_send()

    others(drain)
    each(0, s - 1, lambda o: src_copy(nearest(o)).wait_send())


def on_device(shape, star_pos, star_vel, star_acc, star_jerk, star_mass, star_level,
              active_index, active_count):
    del active_count
    n_ia, n_ja, s = shape
    t = n_ia * (n_ja // s)
    stars = star_mass.shape[0]
    cap = active_index.shape[0]
    f32 = jnp.float32
    return pl.pallas_call(
        functools.partial(kernel, shape),
        out_shape=pltpu.VMEM((cap, 12), f32),
        in_specs=[pl.BlockSpec(memory_space=pltpu.HBM)] * 7,
        out_specs=pl.BlockSpec(memory_space=pltpu.VMEM),
        scratch_shapes=[
            pltpu.VMEM((3, stars), f32), pltpu.VMEM((3, stars), f32),
            pltpu.VMEM((3, stars), f32), pltpu.VMEM((3, stars), f32),
            pltpu.VMEM((1, stars), f32), pltpu.VMEM((1, stars), jnp.int32),
            pltpu.SMEM((cap,), jnp.int32),
            pltpu.VMEM((s, 8, stars), f32),
            pltpu.VMEM((t, cap, LANES), f32),
            pltpu.VMEM((t, 6, cap, LANES), f32),
            pltpu.VMEM((t, 6, cap, LANES), f32),
            pltpu.VMEM((t, cap, LANES), f32),
            pltpu.VMEM((t, cap, LANES), f32),
            pltpu.SemaphoreType.DMA((7,)),
            pltpu.SemaphoreType.DMA((s,)), pltpu.SemaphoreType.DMA((s,)),
            pltpu.SemaphoreType.DMA((t,)), pltpu.SemaphoreType.DMA((t,)),
            pltpu.SemaphoreType.DMA((t,)), pltpu.SemaphoreType.DMA((t,)),
            pltpu.SemaphoreType.REGULAR((s,)),
        ],
        compiler_params=pltpu.CompilerParams(collective_id=0, has_side_effects=True),
    )(star_pos, star_vel, star_acc, star_jerk, star_mass.reshape(1, stars),
      star_level.reshape(1, stars), active_index).T


def solution(mesh):
    n_ia, n_ja = mesh.shape["ia"], mesh.shape["ja"]
    s = SOURCE_PARTS if n_ja % SOURCE_PARTS == 0 else 1
    columns = P(None, ("ia", "ja"))
    flat = P(("ia", "ja"))
    return jax.shard_map(
        functools.partial(on_device, (n_ia, n_ja, s)), mesh=mesh,
        in_specs=(columns,) * 4 + (flat,) * 4, out_specs=columns, check_vma=False)
```

```python
import functools

import jax
import jax.numpy as jnp
from jax import lax
from jax.experimental import pallas as pl
from jax.experimental.pallas import tpu as pltpu
from jax.sharding import PartitionSpec as P

tick_now = 44
top_level = 5
tick_length = 0.125
soft_square = 0.0001
first_active_level = 3

LANES = 128
SOURCE_PARTS = 4
FAR = 64


def kernel(
    shape, pos_hbm, vel_hbm, acc_hbm, jerk_hbm, mass_hbm, level_hbm, idx_hbm, out_ref,
    big, mass, level, idx, src, tgt, wide, sums, part, got,
    in_sem, src_send, src_recv, tgt_send, tgt_recv, red_send, red_recv, ready, mates,
):
    n_ia, n_ja, s = shape
    n_lo = n_ja // s
    t = n_ia * n_lo
    flip = n_ia % 2 == 0
    pair = 2 if t % 2 == 0 else 1
    stars = mass.shape[1]
    cap = idx.shape[0]
    ia, ja = lax.axis_index("ia"), lax.axis_index("ja")
    hi, lo = ja // n_lo, ja % n_lo
    me = lo * n_ia + ia
    mesh_id = pl.DeviceIdType.MESH

    def mate(p):
        return (p % n_ia, hi * n_lo + p // n_ia)

    def partner(o):
        other = ia + 1 - 2 * (ia % 2) if flip else ia
        return (other, o * n_lo + lo)

    def nearest(o):
        up = o + jnp.where(o >= hi, 1, 0)
        down = s - 1 - o - jnp.where(o >= s - 1 - hi, 1, 0)
        return jnp.where(2 * hi < s, up, down)

    def src_copy(o):
        return pltpu.make_async_remote_copy(
            src_ref=src.at[hi], dst_ref=src.at[hi], send_sem=src_send,
            recv_sem=src_recv.at[hi], device_id=partner(o), device_id_type=mesh_id)

    def tgt_copy(p):
        return pltpu.make_async_remote_copy(
            src_ref=tgt.at[me], dst_ref=tgt.at[me], send_sem=tgt_send,
            recv_sem=tgt_recv.at[jnp.where(me < pair, 0, 1)], device_id=mate(p),
            device_id_type=mesh_id)

    def red_copy(p):
        return pltpu.make_async_remote_copy(
            src_ref=part.at[p], dst_ref=got.at[me], send_sem=red_send,
            recv_sem=red_recv, device_id=mate(p), device_id_type=mesh_id)

    def wait_for(ref, n, sem):
        if n > 0:
            pltpu.make_async_copy(ref.at[0:n], ref.at[0:n], sem).wait()

    def each(low, high, body):
        def step(k, carry):
            body(k)
            return carry
        lax.fori_loop(low, high, step, 0)

    def others(body):
        def step(p):
            @pl.when(p != me)
            def other():
                body(p)
        each(0, t, step)

    barrier = pltpu.get_barrier_semaphore()

    def signal(semaphore, device):
        pl.semaphore_signal(semaphore, inc=1, device_id=device, device_id_type=mesh_id)

    loads = [
        pltpu.make_async_copy(a, b, in_sem.at[i])
        for i, a, b in [
            (0, pos_hbm, big.at[0]), (0, vel_hbm, big.at[1]), (0, acc_hbm, big.at[2]),
            (0, jerk_hbm, big.at[3]), (1, level_hbm, level), (2, mass_hbm, mass),
            (3, idx_hbm, idx)]
    ]
    for load in loads:
        load.start()

    each(hi + 1, s, lambda o: signal(barrier, partner(o)))
    each(me + 1, t, lambda p: signal(barrier, mate(p)))

    @pl.when(hi == 0)
    def greet_near():
        each(0, me, lambda p: signal(barrier, mate(p)))

    @pl.when(hi > 0)
    def answer():
        pl.semaphore_wait(barrier, hi + me)
        each(0, hi, lambda o: signal(ready.at[hi], partner(o)))
        each(0, me, lambda p: signal(mates, mate(p)))

    wait_for(big, 4, in_sem.at[0])
    loads[4].wait()
    loads[5].wait()

    pos, vel, acc, jerk = [big[i] for i in range(4)]
    periods = jnp.left_shift(jnp.ones((1, stars), jnp.int32), top_level - level[...])
    remains = jnp.bitwise_and(tick_now, periods - 1)
    age = jnp.where(remains == 0, periods, remains).astype(jnp.float32) * tick_length
    src[hi, 0:3] = pos + age * (vel + age * (acc * 0.5 + age * jerk * (1.0 / 6.0)))
    src[hi, 3:6] = vel + age * (acc + age * jerk * 0.5)
    src[hi, 6:7] = mass[...]
    src[hi, 7:8] = age
    each(0, hi, lambda o: src_copy(o).start())

    loads[6].wait()
    slot = lax.broadcasted_iota(jnp.int32, (cap, stars), 0)
    want = jnp.zeros((cap, stars), jnp.int32)
    for i in range(cap):
        want = jnp.where(slot == i, idx[i], want)
    mask = lax.broadcasted_iota(jnp.int32, (cap, stars), 1) == want

    def pick(row):
        return jnp.sum(jnp.where(mask, row, 0.0), axis=1, keepdims=True)

    lane = lax.broadcasted_iota(jnp.int32, (cap, LANES), 1)

    def columns(values):
        tile = jnp.zeros((cap, LANES), jnp.float32)
        for i, value in values:
            tile = jnp.where(lane == i, value, tile)
        return tile

    own = [pick(src[hi, q:q + 1]) for q in range(6)]
    tgt[me] = columns(enumerate(own))

    @pl.when(hi == 0)
    def all_here():
        pl.semaphore_wait(barrier, t - 1)

    @pl.when((hi > 0) & (me < t - 1))
    def far_here():
        pl.semaphore_wait(mates, t - 1 - me)

    others(lambda p: tgt_copy(p).start())

    old_acc = [pick(big[2, q:q + 1, :]) for q in range(3)]
    old_jerk = [pick(big[3, q:q + 1, :]) for q in range(3)]
    h = pick(src[hi, 7:8])
    live = pick(level[...].astype(jnp.float32)) > first_active_level - 0.5
    h2 = h * h
    fixed = [own[q] - h2 * (0.15 * old_acc[q] + (7.0 / 60.0) * h * old_jerk[q])
             for q in range(3)]
    fixed += [own[3 + q] - h * (0.5 * old_acc[q] + (5.0 / 12.0) * h * old_jerk[q])
              for q in range(3)]
    constant = columns(enumerate(fixed))
    factor = columns([(q, 0.15 * h2) for q in range(3)] + [(3 + q, 0.5 * h) for q in range(3)]
                     + [(6 + q, 1.0) for q in range(6)]
                     + [(FAR + q, h2 * h * (-1.0 / 30.0)) for q in range(3)]
                     + [(FAR + 3 + q, h2 * (-1.0 / 12.0)) for q in range(3)])

    kind = jnp.full((cap, LANES), -1, jnp.int32)
    for i in range(9):
        kind = jnp.where(lane == i, i % 3, kind)
    for q in range(3):
        kind = jnp.where(lane == 9 + q, 3 + q, kind)
    for i in range(6):
        kind = jnp.where(lane == FAR + i, 3 + i % 3, kind)

    def reply(o):
        pl.semaphore_wait(ready.at[o], 1)
        src_copy(o).start()

    each(hi + 1, s, reply)

    def pairs(targets, j, totals):
        totals = [list(total) for total in totals]
        for c in range(stars // LANES):
            row = [src[j, q:q + 1, c * LANES:(c + 1) * LANES] for q in range(7)]
            for target, total in zip(targets, totals):
                d = [row[q] - target[q] for q in range(3)]
                w = [row[3 + q] - target[3 + q] for q in range(3)]
                u = lax.rsqrt(d[0] * d[0] + d[1] * d[1] + d[2] * d[2] + soft_square)
                u2 = u * u
                m = row[6] * u * u2
                r = 3.0 * (d[0] * w[0] + d[1] * w[1] + d[2] * w[2]) * u2
                for q in range(3):
                    total[q] = total[q] + m * d[q]
                    total[3 + q] = total[3 + q] + m * (w[q] - r * d[q])
        return totals

    def spread(k):
        tile = tgt[k]
        return [jnp.broadcast_to(tile[:, q:q + 1], (cap, LANES)) for q in range(6)]

    def zeros():
        return [[jnp.zeros((cap, LANES), jnp.float32)] * 6 for _ in range(pair)]

    def first(i):
        ks = [i * pair + b for b in range(pair)]
        targets = [spread(k) for k in ks]
        totals = pairs(targets, hi, zeros())
        for k, target, total in zip(ks, targets, totals):
            for q in range(6):
                wide[k, q] = target[q]
                sums[k, q] = total[q]

    def finish(i, totals):
        ks = [i * pair + b for b in range(pair)]
        forces = [[jnp.sum(x, axis=1, keepdims=True) for x in total] for total in totals]
        for k, force in zip(ks, forces):
            tile = jnp.zeros((cap, LANES), jnp.float32)
            for q in range(6):
                tile = jnp.where(kind == q, force[q], tile)
            part[k] = tile
        for k in ks:
            @pl.when(k != me)
            def send(k=k):
                red_copy(k).start()

    def rest(i):
        ks = [i * pair + b for b in range(pair)]
        targets = [[wide[k, q] for q in range(6)] for k in ks]
        totals = [[sums[k, q] for q in range(6)] for k in ks]
        finish(i, lax.fori_loop(
            0, s - 1, lambda o, totals: pairs(targets, nearest(o), totals), totals))

    def arrival(o):
        j = nearest(o)
        pltpu.make_async_copy(src.at[j], src.at[j], src_recv.at[j]).wait()
        return j

    @pl.when(me < pair)
    def other_pairs_near():
        wait_for(tgt, t - pair, tgt_recv.at[1])

    @pl.when(me >= pair)
    def other_pairs_far():
        wait_for(tgt, t - pair - 1, tgt_recv.at[1])

    each(1, t // pair, first)

    @pl.when(me < pair)
    def first_pair_near():
        wait_for(tgt, pair - 1, tgt_recv.at[0])

    @pl.when(me >= pair)
    def first_pair_far():
        wait_for(tgt, pair, tgt_recv.at[0])

    targets = [spread(k) for k in range(pair)]
    totals = pairs(targets, hi, zeros())
    finish(0, lax.fori_loop(
        0, s - 1, lambda o, totals: pairs(targets, arrival(o), totals), totals))
    each(1, t // pair, rest)
    got[me] = part[me]

    wait_for(got, t - 1, red_recv)
    total = lax.fori_loop(0, t, lambda p, total: total + got[p],
                          jnp.zeros((cap, LANES), jnp.float32)) * factor
    result = constant + total + pltpu.roll(total, LANES - FAR, 1)
    out_ref[...] = jnp.where(live, result, 0.0)[:, :12]

    wait_for(part, t - 1, red_send)
    wait_for(tgt, t - 1, tgt_send)
    wait_for(src, s - 1, src_send)


def on_device(shape, star_pos, star_vel, star_acc, star_jerk, star_mass, star_level,
              active_index, active_count):
    del active_count
    n_ia, n_ja, s = shape
    t = n_ia * (n_ja // s)
    stars = star_mass.shape[0]
    cap = active_index.shape[0]
    f32 = jnp.float32
    return pl.pallas_call(
        functools.partial(kernel, shape),
        out_shape=pltpu.VMEM((cap, 12), f32),
        in_specs=[pl.BlockSpec(memory_space=pltpu.HBM)] * 7,
        out_specs=pl.BlockSpec(memory_space=pltpu.VMEM),
        scratch_shapes=[
            pltpu.VMEM((4, 3, stars), f32),
            pltpu.VMEM((1, stars), f32), pltpu.VMEM((1, stars), jnp.int32),
            pltpu.SMEM((cap,), jnp.int32),
            pltpu.VMEM((s, 8, stars), f32),
            pltpu.VMEM((t, cap, LANES), f32),
            pltpu.VMEM((t, 6, cap, LANES), f32),
            pltpu.VMEM((t, 6, cap, LANES), f32),
            pltpu.VMEM((t, cap, LANES), f32),
            pltpu.VMEM((t, cap, LANES), f32),
            pltpu.SemaphoreType.DMA((4,)),
            pltpu.SemaphoreType.DMA, pltpu.SemaphoreType.DMA((s,)),
            pltpu.SemaphoreType.DMA, pltpu.SemaphoreType.DMA((2,)),
            pltpu.SemaphoreType.DMA, pltpu.SemaphoreType.DMA,
            pltpu.SemaphoreType.REGULAR((s,)), pltpu.SemaphoreType.REGULAR,
        ],
        compiler_params=pltpu.CompilerParams(collective_id=0, has_side_effects=True),
    )(star_pos, star_vel, star_acc, star_jerk, star_mass.reshape(1, stars),
      star_level.reshape(1, stars), active_index).T


def solution(mesh):
    n_ia, n_ja = mesh.shape["ia"], mesh.shape["ja"]
    s = SOURCE_PARTS if n_ja % SOURCE_PARTS == 0 else 1
    columns = P(None, ("ia", "ja"))
    flat = P(("ia", "ja"))
    return jax.shard_map(
        functools.partial(on_device, (n_ia, n_ja, s)), mesh=mesh,
        in_specs=(columns,) * 4 + (flat,) * 4, out_specs=columns, check_vma=False)
```

```python
import functools

import jax
import jax.numpy as jnp
from jax import lax
from jax.experimental import pallas as pl
from jax.experimental.pallas import tpu as pltpu
from jax.sharding import PartitionSpec as P

tick_now = 44
top_level = 5
tick_length = 0.125
soft_square = 0.0001
first_active_level = 3

LANES = 128
SOURCE_PARTS = 4
FAR = 64


def kernel(
    shape, pos_hbm, vel_hbm, acc_hbm, jerk_hbm, mass_hbm, level_hbm, idx_hbm, out_ref,
    big, mass, level, idx, src, tgt, wide, sums, part, got,
    in_sem, src_send, src_recv, tgt_send, tgt_recv, red_send, red_recv, ready, mates,
):
    n_ia, n_ja, s = shape
    n_lo = n_ja // s
    t = n_ia * n_lo
    flip = n_ia % 2 == 0
    pair = 2 if t % 2 == 0 else 1
    corner = s > 1 and t >= 2 * pair
    stars = mass.shape[1]
    cap = idx.shape[0]
    ia, ja = lax.axis_index("ia"), lax.axis_index("ja")
    hi, lo = ja // n_lo, ja % n_lo
    me = lo * n_ia + ia
    mesh_id = pl.DeviceIdType.MESH

    home = (hi == 0) & (me < pair) & corner
    remote = (hi == s - 1) & (me >= t - pair) & corner
    between = (hi == 0) & (me >= t - pair) & corner

    chip = 2 if flip else 1

    def distance(p):
        return p // n_ia + (p % n_ia) // chip

    mine = distance(me)
    side = n_ia // chip
    nearer = sum(chip * jnp.clip(mine - k, 0, side) for k in range(n_lo)) + me % chip
    farther = sum(chip * (side - jnp.clip(mine - k + 1, 0, side)) for k in range(n_lo))
    farther = farther + chip - 1 - me % chip

    def beyond(p):
        return (distance(p) > mine) | ((p // chip == me // chip) & (p > me))

    def before(p):
        return (distance(p) < mine) | ((p // chip == me // chip) & (p < me))

    def mate(p):
        return (p % n_ia, hi * n_lo + p // n_ia)

    def partner(o):
        other = ia + 1 - 2 * (ia % 2) if flip else ia
        return (other, o * n_lo + lo)

    def nearest(o):
        up = o + jnp.where(o >= hi, 1, 0)
        down = s - 1 - o - jnp.where(o >= s - 1 - hi, 1, 0)
        return jnp.where(2 * hi < s, up, down)

    def src_copy(o):
        return pltpu.make_async_remote_copy(
            src_ref=src.at[hi], dst_ref=src.at[hi], send_sem=src_send,
            recv_sem=src_recv.at[hi], device_id=partner(o), device_id_type=mesh_id)

    def corner_of():
        p = t - 1 - me
        return (p % n_ia, jnp.where(hi == 0, s - 1, 0) * n_lo + p // n_ia)

    def corner_copy():
        return pltpu.make_async_remote_copy(
            src_ref=src.at[hi], dst_ref=src.at[s], send_sem=src_send,
            recv_sem=src_recv.at[s], device_id=corner_of(), device_id_type=mesh_id)

    def tgt_copy(p):
        return pltpu.make_async_remote_copy(
            src_ref=tgt.at[me], dst_ref=tgt.at[me], send_sem=tgt_send,
            recv_sem=tgt_recv.at[jnp.where(me < pair, 0, 1)], device_id=mate(p),
            device_id_type=mesh_id)

    def red_copy(p):
        return pltpu.make_async_remote_copy(
            src_ref=part.at[p], dst_ref=got.at[me], send_sem=red_send,
            recv_sem=red_recv, device_id=mate(p), device_id_type=mesh_id)

    def wait_for(ref, n, sem):
        if n > 0:
            pltpu.make_async_copy(ref.at[0:n], ref.at[0:n], sem).wait()

    def each(low, high, body):
        def step(k, carry):
            body(k)
            return carry
        lax.fori_loop(low, high, step, 0)

    def others(body):
        def step(p):
            @pl.when(p != me)
            def other():
                body(p)
        each(0, t, step)

    barrier = pltpu.get_barrier_semaphore()

    def signal(semaphore, device):
        pl.semaphore_signal(semaphore, inc=1, device_id=device, device_id_type=mesh_id)

    loads = [
        pltpu.make_async_copy(a, b, in_sem.at[i])
        for i, a, b in [
            (0, pos_hbm, big.at[0]), (0, vel_hbm, big.at[1]), (0, acc_hbm, big.at[2]),
            (0, jerk_hbm, big.at[3]), (1, level_hbm, level), (2, mass_hbm, mass),
            (3, idx_hbm, idx)]
    ]
    for load in loads:
        load.start()

    each(hi + 1, s, lambda o: signal(barrier, partner(o)))

    @pl.when(home)
    def greet_corner():
        signal(barrier, corner_of())

    def greet(p):
        @pl.when((hi == 0) | beyond(p))
        def hello():
            signal(barrier, mate(p))

    others(greet)

    @pl.when(hi > 0)
    def answer():
        pl.semaphore_wait(barrier, hi + nearer + jnp.where(remote, 1, 0))
        each(0, hi, lambda o: signal(ready.at[hi], partner(o)))

        def tell(p):
            @pl.when(before(p))
            def back():
                signal(mates, mate(p))

        others(tell)

    wait_for(big, 4, in_sem.at[0])
    loads[4].wait()
    loads[5].wait()

    pos, vel, acc, jerk = [big[i] for i in range(4)]
    periods = jnp.left_shift(jnp.ones((1, stars), jnp.int32), top_level - level[...])
    remains = jnp.bitwise_and(tick_now, periods - 1)
    age = jnp.where(remains == 0, periods, remains).astype(jnp.float32) * tick_length
    src[hi, 0:3] = pos + age * (vel + age * (acc * 0.5 + age * jerk * (1.0 / 6.0)))
    src[hi, 3:6] = vel + age * (acc + age * jerk * 0.5)
    src[hi, 6:7] = mass[...]

    @pl.when(remote)
    def to_home():
        corner_copy().start()

    @pl.when(hi > 0)
    def to_first_part():
        src_copy(0).start()

    loads[6].wait()
    slot = lax.broadcasted_iota(jnp.int32, (cap, stars), 0)
    want = jnp.zeros((cap, stars), jnp.int32)
    for i in range(cap):
        want = jnp.where(slot == i, idx[i], want)
    mask = lax.broadcasted_iota(jnp.int32, (cap, stars), 1) == want

    def pick(row):
        return jnp.sum(jnp.where(mask, row, 0.0), axis=1, keepdims=True)

    lane = lax.broadcasted_iota(jnp.int32, (cap, LANES), 1)

    def columns(values):
        tile = jnp.zeros((cap, LANES), jnp.float32)
        for i, value in values:
            tile = jnp.where(lane == i, value, tile)
        return tile

    own = [pick(src[hi, q:q + 1]) for q in range(6)]
    tgt[me] = columns(enumerate(own))

    each(1, hi, lambda o: src_copy(o).start())

    early = jnp.where((hi > 0) & (mine == 0), s, hi + 1)

    def reply(o):
        pl.semaphore_wait(ready.at[o], 1)
        src_copy(o).start()

    each(hi + 1, early, reply)

    @pl.when(hi == 0)
    def all_here():
        pl.semaphore_wait(barrier, t - 1)

    @pl.when((hi > 0) & (farther > 0))
    def far_here():
        pl.semaphore_wait(mates, farther)

    others(lambda p: tgt_copy(p).start())

    old_acc = [pick(big[2, q:q + 1, :]) for q in range(3)]
    old_jerk = [pick(big[3, q:q + 1, :]) for q in range(3)]
    h = pick(age)
    live = pick(level[...].astype(jnp.float32)) > first_active_level - 0.5
    h2 = h * h
    fixed = [own[q] - h2 * (0.15 * old_acc[q] + (7.0 / 60.0) * h * old_jerk[q])
             for q in range(3)]
    fixed += [own[3 + q] - h * (0.5 * old_acc[q] + (5.0 / 12.0) * h * old_jerk[q])
              for q in range(3)]
    constant = columns(enumerate(fixed))
    factor = columns([(q, 0.15 * h2) for q in range(3)] + [(3 + q, 0.5 * h) for q in range(3)]
                     + [(6 + q, 1.0) for q in range(6)]
                     + [(FAR + q, h2 * h * (-1.0 / 30.0)) for q in range(3)]
                     + [(FAR + 3 + q, h2 * (-1.0 / 12.0)) for q in range(3)])

    kind = jnp.full((cap, LANES), -1, jnp.int32)
    for i in range(9):
        kind = jnp.where(lane == i, i % 3, kind)
    for q in range(3):
        kind = jnp.where(lane == 9 + q, 3 + q, kind)
    for i in range(6):
        kind = jnp.where(lane == FAR + i, 3 + i % 3, kind)

    each(early, s, reply)

    def pairs(targets, j, totals):
        totals = [list(total) for total in totals]
        for c in range(stars // LANES):
            row = [src[j, q:q + 1, c * LANES:(c + 1) * LANES] for q in range(7)]
            for target, total in zip(targets, totals):
                d = [row[q] - target[q] for q in range(3)]
                w = [row[3 + q] - target[3 + q] for q in range(3)]
                u = lax.rsqrt(d[0] * d[0] + d[1] * d[1] + d[2] * d[2] + soft_square)
                u2 = u * u
                m = row[6] * u * u2
                r = 3.0 * (d[0] * w[0] + d[1] * w[1] + d[2] * w[2]) * u2
                for q in range(3):
                    total[q] = total[q] + m * d[q]
                    total[3 + q] = total[3 + q] + m * (w[q] - r * d[q])
        return totals

    def spread(k):
        tile = tgt[k]
        return [jnp.broadcast_to(tile[:, q:q + 1], (cap, LANES)) for q in range(6)]

    def zeros():
        return [[jnp.zeros((cap, LANES), jnp.float32)] * 6 for _ in range(pair)]

    def first(i):
        ks = [i * pair + b for b in range(pair)]
        targets = [spread(k) for k in ks]
        totals = pairs(targets, hi, zeros())
        for k, target, total in zip(ks, targets, totals):
            for q in range(6):
                wide[k, q] = target[q]
                sums[k, q] = total[q]

    def held(i):
        ks = [i * pair + b for b in range(pair)]
        return [[sums[k, q] for q in range(6)] for k in ks]

    def added(i, j):
        ks = [i * pair + b for b in range(pair)]
        return pairs([[wide[k, q] for q in range(6)] for k in ks], j, held(i))

    def add(i, j):
        for b, total in enumerate(added(i, j)):
            for q in range(6):
                sums[i * pair + b, q] = total[q]

    def finish(i, totals):
        ks = [i * pair + b for b in range(pair)]
        forces = [[jnp.sum(x, axis=1, keepdims=True) for x in total] for total in totals]
        for k, force in zip(ks, forces):
            tile = jnp.zeros((cap, LANES), jnp.float32)
            for q in range(6):
                tile = jnp.where(kind == q, force[q], tile)
            part[k] = tile
        for k in ks:
            @pl.when(k != me)
            def send(k=k):
                red_copy(k).start()

    def arrival(j):
        pltpu.make_async_copy(src.at[j], src.at[j], src_recv.at[j]).wait()

    @pl.when(me < pair)
    def other_pairs_near():
        wait_for(tgt, t - pair, tgt_recv.at[1])

    @pl.when(me >= pair)
    def other_pairs_far():
        wait_for(tgt, t - pair - 1, tgt_recv.at[1])

    each(1, t // pair, first)

    @pl.when(me < pair)
    def first_pair_near():
        wait_for(tgt, pair - 1, tgt_recv.at[0])

    @pl.when(me >= pair)
    def first_pair_far():
        wait_for(tgt, pair, tgt_recv.at[0])

    first(0)

    ahead = jnp.where(hi > 0, min(s - 2, 1), 0) if s > 2 else 0

    def near_block(o):
        j = nearest(o)
        arrival(j)
        add(0, j)
        each(1, jnp.where(o < ahead, t // pair, 1), lambda i: add(i, j))

    each(0, s - 2, near_block)
    end = nearest(s - 2) if s > 1 else hi

    if s > 1:
        @pl.when(jnp.logical_not(between))
        def last_block():
            arrival(end)
            add(0, end)

    @pl.when(jnp.logical_not(home))
    def first_pair():
        finish(0, held(0))

    each(1, t // pair, lambda i: each(ahead, s - 2, lambda o: add(i, nearest(o))))
    if corner:
        @pl.when(between)
        def last_arrival():
            arrival(end)

    each(1, t // pair, lambda i: finish(i, added(i, end) if s > 1 else held(i)))

    if corner:
        @pl.when(home)
        def corner_block():
            arrival(s)
            finish(0, added(0, s))

    got[me] = part[me]

    wait_for(got, t - 1, red_recv)
    total = lax.fori_loop(0, t, lambda p, total: total + got[p],
                          jnp.zeros((cap, LANES), jnp.float32)) * factor
    result = constant + total + pltpu.roll(total, LANES - FAR, 1)
    out_ref[...] = jnp.where(live, result, 0.0)[:, :12]

    wait_for(part, t - 1, red_send)
    wait_for(tgt, t - 1, tgt_send)

    @pl.when(remote)
    def sent_corner():
        wait_for(src, s, src_send)

    @pl.when(jnp.logical_not(remote))
    def sent():
        wait_for(src, s - 1, src_send)


def on_device(shape, star_pos, star_vel, star_acc, star_jerk, star_mass, star_level,
              active_index, active_count):
    del active_count
    n_ia, n_ja, s = shape
    t = n_ia * (n_ja // s)
    stars = star_mass.shape[0]
    cap = active_index.shape[0]
    f32 = jnp.float32
    return pl.pallas_call(
        functools.partial(kernel, shape),
        out_shape=pltpu.VMEM((cap, 12), f32),
        in_specs=[pl.BlockSpec(memory_space=pltpu.HBM)] * 7,
        out_specs=pl.BlockSpec(memory_space=pltpu.VMEM),
        scratch_shapes=[
            pltpu.VMEM((4, 3, stars), f32),
            pltpu.VMEM((1, stars), f32), pltpu.VMEM((1, stars), jnp.int32),
            pltpu.SMEM((cap,), jnp.int32),
            pltpu.VMEM((s + 1, 7, stars), f32),
            pltpu.VMEM((t, cap, LANES), f32),
            pltpu.VMEM((t, 6, cap, LANES), f32),
            pltpu.VMEM((t, 6, cap, LANES), f32),
            pltpu.VMEM((t, cap, LANES), f32),
            pltpu.VMEM((t, cap, LANES), f32),
            pltpu.SemaphoreType.DMA((4,)),
            pltpu.SemaphoreType.DMA, pltpu.SemaphoreType.DMA((s + 1,)),
            pltpu.SemaphoreType.DMA, pltpu.SemaphoreType.DMA((2,)),
            pltpu.SemaphoreType.DMA, pltpu.SemaphoreType.DMA,
            pltpu.SemaphoreType.REGULAR((s,)), pltpu.SemaphoreType.REGULAR,
        ],
        compiler_params=pltpu.CompilerParams(collective_id=0, has_side_effects=True),
    )(star_pos, star_vel, star_acc, star_jerk, star_mass.reshape(1, stars),
      star_level.reshape(1, stars), active_index).T


def solution(mesh):
    n_ia, n_ja = mesh.shape["ia"], mesh.shape["ja"]
    s = SOURCE_PARTS if n_ja % SOURCE_PARTS == 0 else 1
    columns = P(None, ("ia", "ja"))
    flat = P(("ia", "ja"))
    return jax.shard_map(
        functools.partial(on_device, (n_ia, n_ja, s)), mesh=mesh,
        in_specs=(columns,) * 4 + (flat,) * 4, out_specs=columns, check_vma=False)
```

```python
import functools

import jax
import jax.numpy as jnp
from jax import lax
from jax.experimental import pallas as pl
from jax.experimental.pallas import tpu as pltpu
from jax.sharding import PartitionSpec as P

tick_now = 44
top_level = 5
tick_length = 0.125
soft_square = 0.0001
first_active_level = 3

LANES = 128
SOURCE_PARTS = 4
FAR = 64


def kernel(
    shape, pos_hbm, vel_hbm, acc_hbm, jerk_hbm, mass_hbm, level_hbm, idx_hbm, out_ref,
    big, mass, level, idx, src, tgt, wide, sums, part, got,
    in_sem, src_send, src_recv, tgt_send, tgt_recv, red_send, red_recv, ready, mates,
):
    n_ia, n_ja, s = shape
    n_lo = n_ja // s
    t = n_ia * n_lo
    flip = n_ia % 2 == 0
    pair = 2 if t % 2 == 0 else 1
    corner = s > 1 and t >= 2 * pair
    stars = mass.shape[1]
    cap = idx.shape[0]
    ia, ja = lax.axis_index("ia"), lax.axis_index("ja")
    hi, lo = ja // n_lo, ja % n_lo
    me = lo * n_ia + ia
    mesh_id = pl.DeviceIdType.MESH

    home = (hi == 0) & (me < pair) & corner
    remote = (hi == s - 1) & (me >= t - pair) & corner
    between = (hi == 0) & (me >= t - pair) & corner

    chip = 2 if flip else 1

    def distance(p):
        return p // n_ia + (p % n_ia) // chip

    mine = distance(me)
    side = n_ia // chip
    nearer = sum(chip * jnp.clip(mine - k, 0, side) for k in range(n_lo)) + me % chip
    farther = sum(chip * (side - jnp.clip(mine - k + 1, 0, side)) for k in range(n_lo))
    farther = farther + chip - 1 - me % chip

    def beyond(p):
        return (distance(p) > mine) | ((p // chip == me // chip) & (p > me))

    def before(p):
        return (distance(p) < mine) | ((p // chip == me // chip) & (p < me))

    def mate(p):
        return (p % n_ia, hi * n_lo + p // n_ia)

    def partner(o):
        other = ia + 1 - 2 * (ia % 2) if flip else ia
        return (other, o * n_lo + lo)

    def nearest(o):
        up = o + jnp.where(o >= hi, 1, 0)
        down = s - 1 - o - jnp.where(o >= s - 1 - hi, 1, 0)
        return jnp.where(2 * hi < s, up, down)

    def src_copy(o):
        return pltpu.make_async_remote_copy(
            src_ref=src.at[hi], dst_ref=src.at[hi], send_sem=src_send,
            recv_sem=src_recv.at[hi], device_id=partner(o), device_id_type=mesh_id)

    def corner_of():
        p = t - 1 - me
        return (p % n_ia, jnp.where(hi == 0, s - 1, 0) * n_lo + p // n_ia)

    def corner_copy():
        return pltpu.make_async_remote_copy(
            src_ref=src.at[hi], dst_ref=src.at[s], send_sem=src_send,
            recv_sem=src_recv.at[s], device_id=corner_of(), device_id_type=mesh_id)

    def tgt_copy(p):
        return pltpu.make_async_remote_copy(
            src_ref=tgt.at[me], dst_ref=tgt.at[me], send_sem=tgt_send,
            recv_sem=tgt_recv.at[jnp.where(p // pair == me // pair, 2, jnp.where(me < pair, 0, 1))],
            device_id=mate(p),
            device_id_type=mesh_id)

    def red_copy(p):
        return pltpu.make_async_remote_copy(
            src_ref=part.at[p], dst_ref=got.at[me], send_sem=red_send,
            recv_sem=red_recv, device_id=mate(p), device_id_type=mesh_id)

    def wait_for(ref, n, sem):
        if n > 0:
            pltpu.make_async_copy(ref.at[0:n], ref.at[0:n], sem).wait()

    def each(low, high, body):
        def step(k, carry):
            body(k)
            return carry
        lax.fori_loop(low, high, step, 0)

    def others(body):
        def step(p):
            @pl.when(p != me)
            def other():
                body(p)
        each(0, t, step)

    barrier = pltpu.get_barrier_semaphore()

    def signal(semaphore, device):
        pl.semaphore_signal(semaphore, inc=1, device_id=device, device_id_type=mesh_id)

    loads = [
        pltpu.make_async_copy(a, b, in_sem.at[i])
        for i, a, b in [
            (0, pos_hbm, big.at[0]), (0, vel_hbm, big.at[1]), (0, acc_hbm, big.at[2]),
            (0, jerk_hbm, big.at[3]), (1, level_hbm, level), (2, mass_hbm, mass),
            (3, idx_hbm, idx)]
    ]
    @pl.when(hi == 0)
    def greet_all():
        others(lambda p: signal(barrier, mate(p)))

    for load in loads:
        load.start()

    each(hi + 1, s, lambda o: signal(barrier, partner(o)))

    @pl.when(home)
    def greet_corner():
        signal(barrier, corner_of())

    def greet(p):
        @pl.when((hi > 0) & beyond(p))
        def hello():
            signal(barrier, mate(p))

    others(greet)

    @pl.when(hi > 0)
    def answer():
        pl.semaphore_wait(barrier, hi + nearer + jnp.where(remote, 1, 0))
        each(0, hi, lambda o: signal(ready.at[hi], partner(o)))

        def tell(p):
            @pl.when(before(p))
            def back():
                signal(mates, mate(p))

        others(tell)

    wait_for(big, 4, in_sem.at[0])
    loads[4].wait()
    loads[5].wait()

    pos, vel, acc, jerk = [big[i] for i in range(4)]
    periods = jnp.left_shift(jnp.ones((1, stars), jnp.int32), top_level - level[...])
    remains = jnp.bitwise_and(tick_now, periods - 1)
    age = jnp.where(remains == 0, periods, remains).astype(jnp.float32) * tick_length
    src[hi, 0:3] = pos + age * (vel + age * (acc * 0.5 + age * jerk * (1.0 / 6.0)))
    src[hi, 3:6] = vel + age * (acc + age * jerk * 0.5)
    src[hi, 6:7] = mass[...]

    @pl.when(remote)
    def to_home():
        corner_copy().start()

    @pl.when(hi > 0)
    def to_first_part():
        src_copy(0).start()

    loads[6].wait()
    slot = lax.broadcasted_iota(jnp.int32, (cap, stars), 0)
    want = jnp.zeros((cap, stars), jnp.int32)
    for i in range(cap):
        want = jnp.where(slot == i, idx[i], want)
    mask = lax.broadcasted_iota(jnp.int32, (cap, stars), 1) == want

    def pick(row):
        return jnp.sum(jnp.where(mask, row, 0.0), axis=1, keepdims=True)

    lane = lax.broadcasted_iota(jnp.int32, (cap, LANES), 1)

    def columns(values):
        tile = jnp.zeros((cap, LANES), jnp.float32)
        for i, value in values:
            tile = jnp.where(lane == i, value, tile)
        return tile

    own = [pick(src[hi, q:q + 1]) for q in range(6)]
    tgt[me] = columns(enumerate(own))

    each(1, hi, lambda o: src_copy(o).start())

    early = jnp.where((hi > 0) & (mine == 0), s, hi + 1)

    def reply(o):
        pl.semaphore_wait(ready.at[o], 1)
        src_copy(o).start()

    each(hi + 1, early, reply)

    @pl.when(hi == 0)
    def all_here():
        pl.semaphore_wait(barrier, t - 1)

    @pl.when((hi > 0) & (farther > 0))
    def far_here():
        pl.semaphore_wait(mates, farther)

    others(lambda p: tgt_copy(p).start())

    old_acc = [pick(big[2, q:q + 1, :]) for q in range(3)]
    old_jerk = [pick(big[3, q:q + 1, :]) for q in range(3)]
    h = pick(age)
    live = pick(level[...].astype(jnp.float32)) > first_active_level - 0.5
    h2 = h * h
    fixed = [own[q] - h2 * (0.15 * old_acc[q] + (7.0 / 60.0) * h * old_jerk[q])
             for q in range(3)]
    fixed += [own[3 + q] - h * (0.5 * old_acc[q] + (5.0 / 12.0) * h * old_jerk[q])
              for q in range(3)]
    constant = columns(enumerate(fixed))
    factor = columns([(q, 0.15 * h2) for q in range(3)] + [(3 + q, 0.5 * h) for q in range(3)]
                     + [(6 + q, 1.0) for q in range(6)]
                     + [(FAR + q, h2 * h * (-1.0 / 30.0)) for q in range(3)]
                     + [(FAR + 3 + q, h2 * (-1.0 / 12.0)) for q in range(3)])

    kind = jnp.full((cap, LANES), -1, jnp.int32)
    for i in range(9):
        kind = jnp.where(lane == i, i % 3, kind)
    for q in range(3):
        kind = jnp.where(lane == 9 + q, 3 + q, kind)
    for i in range(6):
        kind = jnp.where(lane == FAR + i, 3 + i % 3, kind)

    def late(i):
        reply(jnp.where((hi == 0) & (i > 1) & (me % chip == 0), s + 1 - i, i))

    each(early, s, late)

    def pairs(targets, j, totals):
        totals = [list(total) for total in totals]
        for c in range(stars // LANES):
            row = [src[j, q:q + 1, c * LANES:(c + 1) * LANES] for q in range(7)]
            for target, total in zip(targets, totals):
                d = [row[q] - target[q] for q in range(3)]
                w = [row[3 + q] - target[3 + q] for q in range(3)]
                u = lax.rsqrt(d[0] * d[0] + d[1] * d[1] + d[2] * d[2] + soft_square)
                u2 = u * u
                m = row[6] * u * u2
                r = 3.0 * (d[0] * w[0] + d[1] * w[1] + d[2] * w[2]) * u2
                for q in range(3):
                    total[q] = total[q] + m * d[q]
                    total[3 + q] = total[3 + q] + m * (w[q] - r * d[q])
        return totals

    def spread(k):
        tile = tgt[k]
        return [jnp.broadcast_to(tile[:, q:q + 1], (cap, LANES)) for q in range(6)]

    def zeros():
        return [[jnp.zeros((cap, LANES), jnp.float32)] * 6 for _ in range(pair)]

    def first(i):
        ks = [i * pair + b for b in range(pair)]
        targets = [spread(k) for k in ks]
        totals = pairs(targets, hi, zeros())
        for k, target, total in zip(ks, targets, totals):
            for q in range(6):
                wide[k, q] = target[q]
                sums[k, q] = total[q]

    def held(i):
        ks = [i * pair + b for b in range(pair)]
        return [[sums[k, q] for q in range(6)] for k in ks]

    def added(i, j):
        ks = [i * pair + b for b in range(pair)]
        return pairs([[wide[k, q] for q in range(6)] for k in ks], j, held(i))

    def add(i, j):
        for b, total in enumerate(added(i, j)):
            for q in range(6):
                sums[i * pair + b, q] = total[q]

    def finish(i, totals):
        ks = [i * pair + b for b in range(pair)]
        forces = [[jnp.sum(x, axis=1, keepdims=True) for x in total] for total in totals]
        for k, force in zip(ks, forces):
            tile = jnp.zeros((cap, LANES), jnp.float32)
            for q in range(6):
                tile = jnp.where(kind == q, force[q], tile)
            part[k] = tile
        for k in ks:
            @pl.when(k != me)
            def send(k=k):
                red_copy(k).start()

    def arrival(j):
        pltpu.make_async_copy(src.at[j], src.at[j], src_recv.at[j]).wait()

    ours = me // pair
    wait_for(tgt, pair - 1, tgt_recv.at[2])
    first(ours)

    @pl.when(ours == 0)
    def other_pairs_near():
        wait_for(tgt, t - pair, tgt_recv.at[1])

    @pl.when(ours > 0)
    def other_pairs_far():
        wait_for(tgt, t - 2 * pair, tgt_recv.at[1])

    def first_of_others(i):
        @pl.when(i != ours)
        def other_pair():
            first(i)

    each(1, t // pair, first_of_others)

    @pl.when(ours > 0)
    def first_pair_far():
        wait_for(tgt, pair, tgt_recv.at[0])
        first(0)

    ahead = jnp.where(hi > 0, min(s - 2, 1), 0) if s > 2 else 0

    def near_block(o):
        j = nearest(o)
        arrival(j)
        add(0, j)
        each(1, jnp.where(o < ahead, t // pair, 1), lambda i: add(i, j))

    each(0, s - 2, near_block)
    end = nearest(s - 2) if s > 1 else hi

    if s > 1:
        @pl.when(jnp.logical_not(between))
        def last_block():
            arrival(end)
            add(0, end)

    @pl.when(jnp.logical_not(home))
    def first_pair():
        finish(0, held(0))

    each(1, t // pair, lambda i: each(ahead, s - 2, lambda o: add(i, nearest(o))))
    if corner:
        @pl.when(between)
        def last_arrival():
            arrival(end)

    each(1, t // pair, lambda i: finish(i, added(i, end) if s > 1 else held(i)))

    if corner:
        @pl.when(home)
        def corner_block():
            arrival(s)
            finish(0, added(0, s))

    got[me] = part[me]

    wait_for(got, t - 1, red_recv)
    total = lax.fori_loop(0, t, lambda p, total: total + got[p],
                          jnp.zeros((cap, LANES), jnp.float32)) * factor
    result = constant + total + pltpu.roll(total, LANES - FAR, 1)
    out_ref[...] = jnp.where(live, result, 0.0)[:, :12]

    wait_for(part, t - 1, red_send)
    wait_for(tgt, t - 1, tgt_send)

    @pl.when(remote)
    def sent_corner():
        wait_for(src, s, src_send)

    @pl.when(jnp.logical_not(remote))
    def sent():
        wait_for(src, s - 1, src_send)


def on_device(shape, star_pos, star_vel, star_acc, star_jerk, star_mass, star_level,
              active_index, active_count):
    del active_count
    n_ia, n_ja, s = shape
    t = n_ia * (n_ja // s)
    stars = star_mass.shape[0]
    cap = active_index.shape[0]
    f32 = jnp.float32
    return pl.pallas_call(
        functools.partial(kernel, shape),
        out_shape=pltpu.VMEM((cap, 12), f32),
        in_specs=[pl.BlockSpec(memory_space=pltpu.HBM)] * 7,
        out_specs=pl.BlockSpec(memory_space=pltpu.VMEM),
        scratch_shapes=[
            pltpu.VMEM((4, 3, stars), f32),
            pltpu.VMEM((1, stars), f32), pltpu.VMEM((1, stars), jnp.int32),
            pltpu.SMEM((cap,), jnp.int32),
            pltpu.VMEM((s + 1, 7, stars), f32),
            pltpu.VMEM((t, cap, LANES), f32),
            pltpu.VMEM((t, 6, cap, LANES), f32),
            pltpu.VMEM((t, 6, cap, LANES), f32),
            pltpu.VMEM((t, cap, LANES), f32),
            pltpu.VMEM((t, cap, LANES), f32),
            pltpu.SemaphoreType.DMA((4,)),
            pltpu.SemaphoreType.DMA, pltpu.SemaphoreType.DMA((s + 1,)),
            pltpu.SemaphoreType.DMA, pltpu.SemaphoreType.DMA((3,)),
            pltpu.SemaphoreType.DMA, pltpu.SemaphoreType.DMA,
            pltpu.SemaphoreType.REGULAR((s,)), pltpu.SemaphoreType.REGULAR,
        ],
        compiler_params=pltpu.CompilerParams(collective_id=0, has_side_effects=True),
    )(star_pos, star_vel, star_acc, star_jerk, star_mass.reshape(1, stars),
      star_level.reshape(1, stars), active_index).T


def solution(mesh):
    n_ia, n_ja = mesh.shape["ia"], mesh.shape["ja"]
    s = SOURCE_PARTS if n_ja % SOURCE_PARTS == 0 else 1
    columns = P(None, ("ia", "ja"))
    flat = P(("ia", "ja"))
    return jax.shard_map(
        functools.partial(on_device, (n_ia, n_ja, s)), mesh=mesh,
        in_specs=(columns,) * 4 + (flat,) * 4, out_specs=columns, check_vma=False)
```

```python
import functools

import jax
import jax.numpy as jnp
from jax import lax
from jax.experimental import pallas as pl
from jax.experimental.pallas import tpu as pltpu
from jax.sharding import PartitionSpec as P

tick_now = 44
top_level = 5
tick_length = 0.125
soft_square = 0.0001
first_active_level = 3

LANES = 128
SOURCE_PARTS = 4
FAR = 64
UNROLLED = 16


def kernel(
    shape, pos_hbm, vel_hbm, acc_hbm, jerk_hbm, mass_hbm, level_hbm, idx_hbm, out_ref,
    big, mass, level, idx, src, tgt, wide, sums, part, got,
    in_sem, src_send, src_recv, tgt_send, tgt_recv, red_send, red_recv, ready, mates,
):
    n_ia, n_ja, s = shape
    n_lo = n_ja // s
    t = n_ia * n_lo
    flip = n_ia % 2 == 0
    pair = 2 if t % 2 == 0 else 1
    corner = s > 1 and t >= 2 * pair
    stars = mass.shape[1]
    cap = idx.shape[0]
    ia, ja = lax.axis_index("ia"), lax.axis_index("ja")
    hi, lo = ja // n_lo, ja % n_lo
    me = lo * n_ia + ia
    mesh_id = pl.DeviceIdType.MESH

    home = (hi == 0) & (me < pair) & corner
    remote = (hi == s - 1) & (me >= t - pair) & corner
    between = (hi == 0) & (me >= t - pair) & corner

    chip = 2 if flip else 1

    def distance(p):
        return p // n_ia + (p % n_ia) // chip

    mine = distance(me)
    side = n_ia // chip
    nearer = sum(chip * jnp.clip(mine - k, 0, side) for k in range(n_lo)) + me % chip
    farther = sum(chip * (side - jnp.clip(mine - k + 1, 0, side)) for k in range(n_lo))
    farther = farther + chip - 1 - me % chip

    def beyond(p):
        return (distance(p) > mine) | ((p // chip == me // chip) & (p > me))

    def before(p):
        return (distance(p) < mine) | ((p // chip == me // chip) & (p < me))

    def mate(p):
        return (p % n_ia, hi * n_lo + p // n_ia)

    def partner(o):
        other = ia + 1 - 2 * (ia % 2) if flip else ia
        return (other, o * n_lo + lo)

    def nearest(o):
        up = o + jnp.where(o >= hi, 1, 0)
        down = s - 1 - o - jnp.where(o >= s - 1 - hi, 1, 0)
        return jnp.where(2 * hi < s, up, down)

    def src_copy(o):
        return pltpu.make_async_remote_copy(
            src_ref=src.at[hi], dst_ref=src.at[hi], send_sem=src_send,
            recv_sem=src_recv.at[hi - jnp.where(hi > o, 1, 0)], device_id=partner(o), device_id_type=mesh_id)

    def corner_of():
        p = t - 1 - me
        return (p % n_ia, jnp.where(hi == 0, s - 1, 0) * n_lo + p // n_ia)

    def corner_copy():
        return pltpu.make_async_remote_copy(
            src_ref=src.at[hi], dst_ref=src.at[s], send_sem=src_send,
            recv_sem=src_recv.at[s - 1], device_id=corner_of(), device_id_type=mesh_id)

    def tgt_copy(p):
        return pltpu.make_async_remote_copy(
            src_ref=tgt.at[me], dst_ref=tgt.at[me], send_sem=tgt_send,
            recv_sem=tgt_recv.at[jnp.where(p // pair == me // pair, 2, jnp.where(me < pair, 0, 1))],
            device_id=mate(p),
            device_id_type=mesh_id)

    def red_copy(p):
        return pltpu.make_async_remote_copy(
            src_ref=part.at[p], dst_ref=got.at[me], send_sem=red_send,
            recv_sem=red_recv, device_id=mate(p), device_id_type=mesh_id)

    def wait_for(ref, n, sem):
        if n > 0:
            pltpu.make_async_copy(ref.at[0:n], ref.at[0:n], sem).wait()

    def each(low, high, body):
        def step(k, carry):
            body(k)
            return carry
        lax.fori_loop(low, high, step, 0)

    def others(body):
        def step(p):
            @pl.when(p != me)
            def other():
                body(p)
        each(0, t, step)

    barrier = pltpu.get_barrier_semaphore()

    def signal(semaphore, device):
        pl.semaphore_signal(semaphore, inc=1, device_id=device, device_id_type=mesh_id)

    loads = [
        pltpu.make_async_copy(a, b, in_sem.at[i])
        for i, a, b in [
            (0, pos_hbm, big.at[0]), (0, vel_hbm, big.at[1]), (0, acc_hbm, big.at[2]),
            (0, jerk_hbm, big.at[3]), (1, level_hbm, level), (2, mass_hbm, mass),
            (3, idx_hbm, idx)]
    ]
    @pl.when(hi == 0)
    def greet_all():
        others(lambda p: signal(barrier, mate(p)))

    for load in loads:
        load.start()

    each(hi + 1, s, lambda o: signal(barrier, partner(o)))

    @pl.when(home)
    def greet_corner():
        signal(barrier, corner_of())

    def greet(p):
        @pl.when((hi > 0) & beyond(p))
        def hello():
            signal(barrier, mate(p))

    others(greet)

    @pl.when(hi > 0)
    def near_here():
        pl.semaphore_wait(barrier, hi + nearer + jnp.where(remote, 1, 0))
        each(0, hi, lambda o: signal(ready.at[hi - 1], partner(o)))

    wait_for(big, 4, in_sem.at[0])
    loads[4].wait()
    loads[5].wait()

    pos, vel, acc, jerk = [big[i] for i in range(4)]
    periods = jnp.left_shift(jnp.ones((1, stars), jnp.int32), top_level - level[...])
    remains = jnp.bitwise_and(tick_now, periods - 1)
    age = jnp.where(remains == 0, periods, remains).astype(jnp.float32) * tick_length
    src[hi, 0:3] = pos + age * (vel + age * (acc * 0.5 + age * jerk * (1.0 / 6.0)))
    src[hi, 3:6] = vel + age * (acc + age * jerk * 0.5)
    src[hi, 6:7] = mass[...]

    @pl.when(remote)
    def to_home():
        corner_copy().start()

    @pl.when(hi > 0)
    def to_first_part():
        src_copy(0).start()

    @pl.when(hi > 0)
    def answer():
        def tell(p):
            @pl.when(before(p))
            def back():
                signal(mates, mate(p))

        others(tell)


    loads[6].wait()
    slot = lax.broadcasted_iota(jnp.int32, (cap, stars), 0)
    want = jnp.zeros((cap, stars), jnp.int32)
    for i in range(cap):
        want = jnp.where(slot == i, idx[i], want)
    mask = lax.broadcasted_iota(jnp.int32, (cap, stars), 1) == want

    def pick(row):
        return jnp.sum(jnp.where(mask, row, 0.0), axis=1, keepdims=True)

    lane = lax.broadcasted_iota(jnp.int32, (cap, LANES), 1)

    def columns(values):
        tile = jnp.zeros((cap, LANES), jnp.float32)
        for i, value in values:
            tile = jnp.where(lane == i, value, tile)
        return tile

    own = [pick(src[hi, q:q + 1]) for q in range(6)]
    tgt[me] = columns(enumerate(own))

    each(1, hi, lambda o: src_copy(o).start())

    early = jnp.where((hi > 0) & (mine == 0), s, hi + 1)

    def reply(o):
        pl.semaphore_wait(ready.at[o - 1], 1)
        src_copy(o).start()

    each(hi + 1, early, reply)

    @pl.when(hi == 0)
    def all_here():
        pl.semaphore_wait(barrier, t - 1)

    @pl.when((hi > 0) & (farther > 0))
    def far_here():
        pl.semaphore_wait(mates, farther)

    others(lambda p: tgt_copy(p).start())

    old_acc = [pick(big[2, q:q + 1, :]) for q in range(3)]
    old_jerk = [pick(big[3, q:q + 1, :]) for q in range(3)]
    h = pick(age)
    live = pick(level[...].astype(jnp.float32)) > first_active_level - 0.5
    h2 = h * h
    fixed = [own[q] - h2 * (0.15 * old_acc[q] + (7.0 / 60.0) * h * old_jerk[q])
             for q in range(3)]
    fixed += [own[3 + q] - h * (0.5 * old_acc[q] + (5.0 / 12.0) * h * old_jerk[q])
              for q in range(3)]
    constant = columns(enumerate(fixed))
    factor = columns([(q, 0.15 * h2) for q in range(3)] + [(3 + q, 0.5 * h) for q in range(3)]
                     + [(6 + q, 1.0) for q in range(6)]
                     + [(FAR + q, h2 * h * (-1.0 / 30.0)) for q in range(3)]
                     + [(FAR + 3 + q, h2 * (-1.0 / 12.0)) for q in range(3)])

    kind = jnp.full((cap, LANES), -1, jnp.int32)
    for i in range(9):
        kind = jnp.where(lane == i, i % 3, kind)
    for q in range(3):
        kind = jnp.where(lane == 9 + q, 3 + q, kind)
    for i in range(6):
        kind = jnp.where(lane == FAR + i, 3 + i % 3, kind)

    def late(i):
        reply(jnp.where((hi == 0) & (i > 1) & (me % chip == 0), s + 1 - i, i))

    each(early, s, late)

    def pairs(targets, j, totals):
        totals = [list(total) for total in totals]
        for c in range(stars // LANES):
            row = [src[j, q:q + 1, c * LANES:(c + 1) * LANES] for q in range(7)]
            for target, total in zip(targets, totals):
                d = [row[q] - target[q] for q in range(3)]
                w = [row[3 + q] - target[3 + q] for q in range(3)]
                u = lax.rsqrt(d[0] * d[0] + d[1] * d[1] + d[2] * d[2] + soft_square)
                u2 = u * u
                m = row[6] * u * u2
                r = 3.0 * (d[0] * w[0] + d[1] * w[1] + d[2] * w[2]) * u2
                for q in range(3):
                    total[q] = total[q] + m * d[q]
                    total[3 + q] = total[3 + q] + m * (w[q] - r * d[q])
        return totals

    def spread(k):
        tile = tgt[k]
        return [jnp.broadcast_to(tile[:, q:q + 1], (cap, LANES)) for q in range(6)]

    def zeros():
        return [[jnp.zeros((cap, LANES), jnp.float32)] * 6 for _ in range(pair)]

    def widen(i):
        for k in [i * pair + b for b in range(pair)]:
            for q, value in enumerate(spread(k)):
                wide[k, q] = value

    def first(i, fresh=True):
        ks = [i * pair + b for b in range(pair)]
        if fresh:
            targets = [spread(k) for k in ks]
            for k, target in zip(ks, targets):
                for q in range(6):
                    wide[k, q] = target[q]
        else:
            targets = [[wide[k, q] for q in range(6)] for k in ks]
        for k, total in zip(ks, pairs(targets, hi, zeros())):
            for q in range(6):
                sums[k, q] = total[q]

    def held(i):
        ks = [i * pair + b for b in range(pair)]
        return [[sums[k, q] for q in range(6)] for k in ks]

    def added(i, j):
        ks = [i * pair + b for b in range(pair)]
        return pairs([[wide[k, q] for q in range(6)] for k in ks], j, held(i))

    def add(i, j):
        for b, total in enumerate(added(i, j)):
            for q in range(6):
                sums[i * pair + b, q] = total[q]

    def finish(i, totals):
        ks = [i * pair + b for b in range(pair)]
        forces = [[jnp.sum(x, axis=1, keepdims=True) for x in total] for total in totals]
        for k, force in zip(ks, forces):
            tile = jnp.zeros((cap, LANES), jnp.float32)
            for q in range(6):
                tile = jnp.where(kind == q, force[q], tile)
            part[k] = tile
        for k in ks:
            @pl.when(k != me)
            def send(k=k):
                red_copy(k).start()

    def arrival(j):
        pltpu.make_async_copy(
            src.at[j], src.at[j], src_recv.at[j - jnp.where(j > hi, 1, 0)]).wait()

    ours = me // pair
    wait_for(tgt, pair - 1, tgt_recv.at[2])
    first(ours)

    few = t <= UNROLLED

    def first_of_others(i):
        @pl.when(i != ours)
        def other_pair():
            first(i, not few)

    turn = jnp.where((hi > 0) & (mine > 0) & (mine < n_lo + n_ia // chip - 2), 0, 1)

    def take(k):
        @pl.when((k == turn) & (ours > 0))
        def first_pair():
            wait_for(tgt, pair, tgt_recv.at[0])
            first(0)

        @pl.when(k != turn)
        def other_pairs():
            @pl.when(ours == 0)
            def near():
                wait_for(tgt, t - pair, tgt_recv.at[1])

            @pl.when(ours > 0)
            def far():
                wait_for(tgt, t - 2 * pair, tgt_recv.at[1])

            if few:
                for i in range(1, t // pair):
                    widen(i)
            each(1, t // pair, first_of_others)

    each(0, 2, take)

    ahead = jnp.where(hi > 0, min(s - 2, 1), 0) if s > 2 else 0

    def near_block(o):
        j = nearest(o)
        arrival(j)
        add(0, j)
        each(1, jnp.where(o < ahead, t // pair, 1), lambda i: add(i, j))

    each(0, s - 2, near_block)
    end = nearest(s - 2) if s > 1 else hi

    if s > 1:
        @pl.when(jnp.logical_not(between))
        def last_block():
            arrival(end)
            add(0, end)

    @pl.when(jnp.logical_not(home))
    def first_pair():
        finish(0, held(0))

    each(1, t // pair, lambda i: each(ahead, s - 2, lambda o: add(i, nearest(o))))
    if corner:
        @pl.when(between)
        def last_arrival():
            arrival(end)

    each(1, t // pair, lambda i: finish(i, added(i, end) if s > 1 else held(i)))

    if corner:
        @pl.when(home)
        def corner_block():
            arrival(s)
            finish(0, added(0, s))

    got[me] = part[me]

    wait_for(got, t - 1, red_recv)
    if t > UNROLLED:
        total = lax.fori_loop(0, t, lambda p, total: total + got[p],
                              jnp.zeros((cap, LANES), jnp.float32)) * factor
    else:
        tiles = [got[p] for p in range(t)]
        while len(tiles) > 1:
            tiles = [sum(tiles[i:i + 2]) for i in range(0, len(tiles), 2)]
        total = tiles[0] * factor
    result = constant + total + pltpu.roll(total, LANES - FAR, 1)
    out_ref[...] = jnp.where(live, result, 0.0)[:, :12]

    wait_for(part, t - 1, red_send)
    wait_for(tgt, t - 1, tgt_send)

    @pl.when(remote)
    def sent_corner():
        wait_for(src, s, src_send)

    @pl.when(jnp.logical_not(remote))
    def sent():
        wait_for(src, s - 1, src_send)


def on_device(shape, star_pos, star_vel, star_acc, star_jerk, star_mass, star_level,
              active_index, active_count):
    del active_count
    n_ia, n_ja, s = shape
    t = n_ia * (n_ja // s)
    stars = star_mass.shape[0]
    cap = active_index.shape[0]
    f32 = jnp.float32
    return pl.pallas_call(
        functools.partial(kernel, shape),
        out_shape=pltpu.VMEM((cap, 12), f32),
        in_specs=[pl.BlockSpec(memory_space=pltpu.HBM)] * 7,
        out_specs=pl.BlockSpec(memory_space=pltpu.VMEM),
        scratch_shapes=[
            pltpu.VMEM((4, 3, stars), f32),
            pltpu.VMEM((1, stars), f32), pltpu.VMEM((1, stars), jnp.int32),
            pltpu.SMEM((cap,), jnp.int32),
            pltpu.VMEM((s + 1, 7, stars), f32),
            pltpu.VMEM((t, cap, LANES), f32),
            pltpu.VMEM((t, 6, cap, LANES), f32),
            pltpu.VMEM((t, 6, cap, LANES), f32),
            pltpu.VMEM((t, cap, LANES), f32),
            pltpu.VMEM((t, cap, LANES), f32),
            pltpu.SemaphoreType.DMA((4,)),
            pltpu.SemaphoreType.DMA, pltpu.SemaphoreType.DMA((s,)),
            pltpu.SemaphoreType.DMA, pltpu.SemaphoreType.DMA((3,)),
            pltpu.SemaphoreType.DMA, pltpu.SemaphoreType.DMA,
            pltpu.SemaphoreType.REGULAR((max(s - 1, 1),)), pltpu.SemaphoreType.REGULAR,
        ],
        compiler_params=pltpu.CompilerParams(collective_id=0, has_side_effects=True),
    )(star_pos, star_vel, star_acc, star_jerk, star_mass.reshape(1, stars),
      star_level.reshape(1, stars), active_index).T


def solution(mesh):
    n_ia, n_ja = mesh.shape["ia"], mesh.shape["ja"]
    s = SOURCE_PARTS if n_ja % SOURCE_PARTS == 0 else 1
    columns = P(None, ("ia", "ja"))
    flat = P(("ia", "ja"))
    return jax.shard_map(
        functools.partial(on_device, (n_ia, n_ja, s)), mesh=mesh,
        in_specs=(columns,) * 4 + (flat,) * 4, out_specs=columns, check_vma=False)
```

```python
import functools

import jax
import jax.numpy as jnp
from jax import lax
from jax.experimental import pallas as pl
from jax.experimental.pallas import tpu as pltpu
from jax.sharding import PartitionSpec as P

tick_now = 44
top_level = 5
tick_length = 0.125
soft_square = 0.0001
first_active_level = 3

LANES = 128
SOURCE_PARTS = 4
FAR = 64
UNROLLED = 16


def kernel(
    shape, pos_hbm, vel_hbm, acc_hbm, jerk_hbm, mass_hbm, level_hbm, idx_hbm, out_ref,
    big, mass, level, idx, src, tgt, wide, sums, part, got,
    in_sem, src_send, src_recv, tgt_send, tgt_recv, red_send, red_recv, ready, mates,
):
    n_ia, n_ja, s = shape
    n_lo = n_ja // s
    t = n_ia * n_lo
    flip = n_ia % 2 == 0
    pair = 2 if t % 2 == 0 else 1
    corner = s > 1 and t >= 2 * pair
    stars = mass.shape[1]
    cap = idx.shape[0]
    ia, ja = lax.axis_index("ia"), lax.axis_index("ja")
    hi, lo = ja // n_lo, ja % n_lo
    me = lo * n_ia + ia
    mesh_id = pl.DeviceIdType.MESH

    home = (hi == 0) & (me < pair) & corner
    remote = (hi == s - 1) & (me >= t - pair) & corner
    between = (hi == 0) & (me >= t - pair) & corner

    chip = 2 if flip else 1

    def distance(p):
        return p // n_ia + (p % n_ia) // chip

    mine = distance(me)
    side = n_ia // chip
    nearer = sum(chip * jnp.clip(mine - k, 0, side) for k in range(n_lo)) + me % chip
    farther = sum(chip * (side - jnp.clip(mine - k + 1, 0, side)) for k in range(n_lo))
    farther = farther + chip - 1 - me % chip

    def beyond(p):
        return (distance(p) > mine) | ((p // chip == me // chip) & (p > me))

    def before(p):
        return (distance(p) < mine) | ((p // chip == me // chip) & (p < me))

    def mate(p):
        return (p % n_ia, hi * n_lo + p // n_ia)

    def partner(o):
        other = ia + 1 - 2 * (ia % 2) if flip else ia
        return (other, o * n_lo + lo)

    def nearest(o):
        up = o + jnp.where(o >= hi, 1, 0)
        down = s - 1 - o - jnp.where(o >= s - 1 - hi, 1, 0)
        return jnp.where(2 * hi < s, up, down)

    def src_copy(o):
        return pltpu.make_async_remote_copy(
            src_ref=src.at[hi], dst_ref=src.at[hi], send_sem=src_send,
            recv_sem=src_recv.at[hi - jnp.where(hi > o, 1, 0)], device_id=partner(o), device_id_type=mesh_id)

    def corner_of():
        p = t - 1 - me
        return (p % n_ia, jnp.where(hi == 0, s - 1, 0) * n_lo + p // n_ia)

    def corner_copy():
        return pltpu.make_async_remote_copy(
            src_ref=src.at[hi], dst_ref=src.at[s], send_sem=src_send,
            recv_sem=src_recv.at[s - 1], device_id=corner_of(), device_id_type=mesh_id)

    def tgt_copy(p):
        return pltpu.make_async_remote_copy(
            src_ref=tgt.at[me], dst_ref=tgt.at[me], send_sem=tgt_send,
            recv_sem=tgt_recv.at[jnp.where(p // pair == me // pair, 2, jnp.where(me < pair, 0, 1))],
            device_id=mate(p),
            device_id_type=mesh_id)

    def red_copy(p):
        return pltpu.make_async_remote_copy(
            src_ref=part.at[p], dst_ref=got.at[me], send_sem=red_send,
            recv_sem=red_recv, device_id=mate(p), device_id_type=mesh_id)

    def wait_for(ref, n, sem):
        if n > 0:
            pltpu.make_async_copy(ref.at[0:n], ref.at[0:n], sem).wait()

    def each(low, high, body):
        def step(k, carry):
            body(k)
            return carry
        lax.fori_loop(low, high, step, 0)

    def others(body):
        def step(p):
            @pl.when(p != me)
            def other():
                body(p)
        each(0, t, step)

    barrier = pltpu.get_barrier_semaphore()

    def signal(semaphore, device):
        pl.semaphore_signal(semaphore, inc=1, device_id=device, device_id_type=mesh_id)

    loads = [
        pltpu.make_async_copy(a, b, in_sem.at[i])
        for i, a, b in [
            (0, pos_hbm, big.at[0]), (0, vel_hbm, big.at[1]), (0, acc_hbm, big.at[2]),
            (0, jerk_hbm, big.at[3]), (1, level_hbm, level), (2, mass_hbm, mass),
            (3, idx_hbm, idx)]
    ]
    @pl.when(hi == 0)
    def greet_all():
        others(lambda p: signal(barrier, mate(p)))

    for load in loads:
        load.start()

    each(hi + 1, s, lambda o: signal(barrier, partner(o)))

    @pl.when(home)
    def greet_corner():
        signal(barrier, corner_of())

    def greet(p):
        @pl.when((hi > 0) & beyond(p))
        def hello():
            signal(barrier, mate(p))

    others(greet)

    @pl.when(hi > 0)
    def near_here():
        pl.semaphore_wait(barrier, hi + nearer + jnp.where(remote, 1, 0))
        each(0, hi, lambda o: signal(ready.at[hi - 1], partner(o)))

    wait_for(big, 4, in_sem.at[0])
    loads[4].wait()
    loads[5].wait()

    pos, vel, acc, jerk = [big[i] for i in range(4)]
    periods = jnp.left_shift(jnp.ones((1, stars), jnp.int32), top_level - level[...])
    remains = jnp.bitwise_and(tick_now, periods - 1)
    age = jnp.where(remains == 0, periods, remains).astype(jnp.float32) * tick_length
    src[hi, 0:3] = pos + age * (vel + age * (acc * 0.5 + age * jerk * (1.0 / 6.0)))
    src[hi, 3:6] = vel + age * (acc + age * jerk * 0.5)
    src[hi, 6:7] = mass[...]

    @pl.when(remote)
    def to_home():
        corner_copy().start()

    @pl.when(hi > 0)
    def to_first_part():
        src_copy(0).start()

    @pl.when(hi > 0)
    def answer():
        def tell(p):
            @pl.when(before(p))
            def back():
                signal(mates, mate(p))

        others(tell)


    loads[6].wait()
    slot = lax.broadcasted_iota(jnp.int32, (cap, stars), 0)
    want = jnp.zeros((cap, stars), jnp.int32)
    for i in range(cap):
        want = jnp.where(slot == i, idx[i], want)
    mask = lax.broadcasted_iota(jnp.int32, (cap, stars), 1) == want

    def pick(row):
        return jnp.sum(jnp.where(mask, row, 0.0), axis=1, keepdims=True)

    lane = lax.broadcasted_iota(jnp.int32, (cap, LANES), 1)

    def columns(values):
        tile = jnp.zeros((cap, LANES), jnp.float32)
        for i, value in values:
            tile = jnp.where(lane == i, value, tile)
        return tile

    own = [pick(src[hi, q:q + 1]) for q in range(6)]
    tgt[me] = columns(enumerate(own))

    each(1, hi, lambda o: src_copy(o).start())

    early = jnp.where((hi > 0) & (mine == 0), s, hi + 1)

    def reply(o):
        pl.semaphore_wait(ready.at[o - 1], 1)
        src_copy(o).start()

    each(hi + 1, early, reply)

    @pl.when(hi == 0)
    def all_here():
        pl.semaphore_wait(barrier, t - 1)

    @pl.when((hi > 0) & (farther > 0))
    def far_here():
        pl.semaphore_wait(mates, farther)

    others(lambda p: tgt_copy(p).start())

    old_acc = [pick(big[2, q:q + 1, :]) for q in range(3)]
    old_jerk = [pick(big[3, q:q + 1, :]) for q in range(3)]
    h = pick(age)
    live = pick(level[...].astype(jnp.float32)) > first_active_level - 0.5
    h2 = h * h
    fixed = [own[q] - h2 * (0.15 * old_acc[q] + (7.0 / 60.0) * h * old_jerk[q])
             for q in range(3)]
    fixed += [own[3 + q] - h * (0.5 * old_acc[q] + (5.0 / 12.0) * h * old_jerk[q])
              for q in range(3)]
    constant = columns(enumerate(fixed))
    factor = columns([(q, 0.15 * h2) for q in range(3)] + [(3 + q, 0.5 * h) for q in range(3)]
                     + [(6 + q, 1.0) for q in range(6)]
                     + [(FAR + q, h2 * h * (-1.0 / 30.0)) for q in range(3)]
                     + [(FAR + 3 + q, h2 * (-1.0 / 12.0)) for q in range(3)])

    kind = jnp.full((cap, LANES), -1, jnp.int32)
    for i in range(9):
        kind = jnp.where(lane == i, i % 3, kind)
    for q in range(3):
        kind = jnp.where(lane == 9 + q, 3 + q, kind)
    for i in range(6):
        kind = jnp.where(lane == FAR + i, 3 + i % 3, kind)

    def late(i):
        reply(jnp.where((hi == 0) & (i > 1) & (me % chip == 0), s + 1 - i, i))

    each(early, s, late)

    def pairs(targets, j, totals):
        totals = [list(total) for total in totals]
        for c in range(stars // LANES):
            row = [src[j, q:q + 1, c * LANES:(c + 1) * LANES] for q in range(7)]
            for target, total in zip(targets, totals):
                d = [row[q] - target[q] for q in range(3)]
                w = [row[3 + q] - target[3 + q] for q in range(3)]
                u = lax.rsqrt(d[0] * d[0] + d[1] * d[1] + d[2] * d[2] + soft_square)
                u2 = u * u
                m = row[6] * u * u2
                r = 3.0 * (d[0] * w[0] + d[1] * w[1] + d[2] * w[2]) * u2
                for q in range(3):
                    total[q] = total[q] + m * d[q]
                    total[3 + q] = total[3 + q] + m * (w[q] - r * d[q])
        return totals

    def spread(k):
        tile = tgt[k]
        return [jnp.broadcast_to(tile[:, q:q + 1], (cap, LANES)) for q in range(6)]

    def zeros():
        return [[jnp.zeros((cap, LANES), jnp.float32)] * 6 for _ in range(pair)]

    def widen(i):
        for k in [i * pair + b for b in range(pair)]:
            for q, value in enumerate(spread(k)):
                wide[k, q] = value

    def first(i, fresh=True):
        ks = [i * pair + b for b in range(pair)]
        if fresh:
            targets = [spread(k) for k in ks]
            for k, target in zip(ks, targets):
                for q in range(6):
                    wide[k, q] = target[q]
        else:
            targets = [[wide[k, q] for q in range(6)] for k in ks]
        for k, total in zip(ks, pairs(targets, hi, zeros())):
            for q in range(6):
                sums[k, q] = total[q]

    def held(i):
        ks = [i * pair + b for b in range(pair)]
        return [[sums[k, q] for q in range(6)] for k in ks]

    def added(i, j):
        ks = [i * pair + b for b in range(pair)]
        return pairs([[wide[k, q] for q in range(6)] for k in ks], j, held(i))

    def add(i, j):
        for b, total in enumerate(added(i, j)):
            for q in range(6):
                sums[i * pair + b, q] = total[q]

    def finish(i, totals):
        ks = [i * pair + b for b in range(pair)]
        forces = [[jnp.sum(x, axis=1, keepdims=True) for x in total] for total in totals]
        for k, force in zip(ks, forces):
            tile = jnp.zeros((cap, LANES), jnp.float32)
            for q in range(6):
                tile = jnp.where(kind == q, force[q], tile)
            part[k] = tile
        for k in ks:
            @pl.when(k != me)
            def send(k=k):
                red_copy(k).start()

    def arrival(j):
        pltpu.make_async_copy(
            src.at[j], src.at[j], src_recv.at[j - jnp.where(j > hi, 1, 0)]).wait()

    ours = me // pair
    wait_for(tgt, pair - 1, tgt_recv.at[2])
    first(ours)

    few = t <= UNROLLED

    def first_of_others(i):
        @pl.when(i != ours)
        def other_pair():
            first(i, not few)

    turn = jnp.where((hi > 0) & (mine > 0) & (mine < n_lo + n_ia // chip - 2), 0, 1)

    def take(k):
        @pl.when((k == turn) & (ours > 0))
        def first_pair():
            wait_for(tgt, pair, tgt_recv.at[0])
            first(0)

        @pl.when(k != turn)
        def other_pairs():
            @pl.when(ours == 0)
            def near():
                wait_for(tgt, t - pair, tgt_recv.at[1])

            @pl.when(ours > 0)
            def far():
                wait_for(tgt, t - 2 * pair, tgt_recv.at[1])

            if few:
                for i in range(1, t // pair):
                    widen(i)
            each(1, t // pair, first_of_others)

    each(0, 2, take)

    def near_block(o):
        j = nearest(o)
        arrival(j)
        add(0, j)

    each(0, s - 2, near_block)
    end = nearest(s - 2) if s > 1 else hi

    if s > 1:
        @pl.when(jnp.logical_not(between))
        def last_block():
            arrival(end)
            add(0, end)

    @pl.when(jnp.logical_not(home))
    def first_pair():
        finish(0, held(0))

    each(1, t // pair, lambda i: each(0, s - 2, lambda o: add(i, nearest(o))))
    if corner:
        @pl.when(between)
        def last_arrival():
            arrival(end)

    each(1, t // pair, lambda i: finish(i, added(i, end) if s > 1 else held(i)))

    if corner:
        @pl.when(home)
        def corner_block():
            arrival(s)
            finish(0, added(0, s))

    got[me] = part[me]

    wait_for(got, t - 1, red_recv)
    if t > UNROLLED:
        total = lax.fori_loop(0, t, lambda p, total: total + got[p],
                              jnp.zeros((cap, LANES), jnp.float32)) * factor
    else:
        tiles = [got[p] for p in range(t)]
        while len(tiles) > 1:
            tiles = [sum(tiles[i:i + 2]) for i in range(0, len(tiles), 2)]
        total = tiles[0] * factor
    result = constant + total + pltpu.roll(total, LANES - FAR, 1)
    out_ref[...] = jnp.where(live, result, 0.0)[:, :12]

    wait_for(part, t - 1, red_send)
    wait_for(tgt, t - 1, tgt_send)

    @pl.when(remote)
    def sent_corner():
        wait_for(src, s, src_send)

    @pl.when(jnp.logical_not(remote))
    def sent():
        wait_for(src, s - 1, src_send)


def on_device(shape, star_pos, star_vel, star_acc, star_jerk, star_mass, star_level,
              active_index, active_count):
    del active_count
    n_ia, n_ja, s = shape
    t = n_ia * (n_ja // s)
    stars = star_mass.shape[0]
    cap = active_index.shape[0]
    f32 = jnp.float32
    return pl.pallas_call(
        functools.partial(kernel, shape),
        out_shape=pltpu.VMEM((cap, 12), f32),
        in_specs=[pl.BlockSpec(memory_space=pltpu.HBM)] * 7,
        out_specs=pl.BlockSpec(memory_space=pltpu.VMEM),
        scratch_shapes=[
            pltpu.VMEM((4, 3, stars), f32),
            pltpu.VMEM((1, stars), f32), pltpu.VMEM((1, stars), jnp.int32),
            pltpu.SMEM((cap,), jnp.int32),
            pltpu.VMEM((s + 1, 7, stars), f32),
            pltpu.VMEM((t, cap, LANES), f32),
            pltpu.VMEM((t, 6, cap, LANES), f32),
            pltpu.VMEM((t, 6, cap, LANES), f32),
            pltpu.VMEM((t, cap, LANES), f32),
            pltpu.VMEM((t, cap, LANES), f32),
            pltpu.SemaphoreType.DMA((4,)),
            pltpu.SemaphoreType.DMA, pltpu.SemaphoreType.DMA((s,)),
            pltpu.SemaphoreType.DMA, pltpu.SemaphoreType.DMA((3,)),
            pltpu.SemaphoreType.DMA, pltpu.SemaphoreType.DMA,
            pltpu.SemaphoreType.REGULAR((max(s - 1, 1),)), pltpu.SemaphoreType.REGULAR,
        ],
        compiler_params=pltpu.CompilerParams(collective_id=0, has_side_effects=True),
    )(star_pos, star_vel, star_acc, star_jerk, star_mass.reshape(1, stars),
      star_level.reshape(1, stars), active_index).T


def solution(mesh):
    n_ia, n_ja = mesh.shape["ia"], mesh.shape["ja"]
    s = SOURCE_PARTS if n_ja % SOURCE_PARTS == 0 else 1
    columns = P(None, ("ia", "ja"))
    flat = P(("ia", "ja"))
    return jax.shard_map(
        functools.partial(on_device, (n_ia, n_ja, s)), mesh=mesh,
        in_specs=(columns,) * 4 + (flat,) * 4, out_specs=columns, check_vma=False)
```

```python
import functools

import jax
import jax.numpy as jnp
from jax import lax
from jax.experimental import pallas as pl
from jax.experimental.pallas import tpu as pltpu
from jax.sharding import PartitionSpec as P

tick_now = 44
top_level = 5
tick_length = 0.125
soft_square = 0.0001
first_active_level = 3

LANES = 128
SOURCE_PARTS = 4
FAR = 64
UNROLLED = 16


def kernel(
    shape, pos_hbm, vel_hbm, acc_hbm, jerk_hbm, mass_hbm, level_hbm, idx_hbm, out_ref,
    big, mass, level, idx, src, tgt, wide, sums, part, got,
    in_sem, src_send, src_recv, tgt_send, tgt_recv, red_send, red_recv, ready, mates,
):
    n_ia, n_ja, s = shape
    n_lo = n_ja // s
    t = n_ia * n_lo
    flip = n_ia % 2 == 0
    pair = 2 if t % 2 == 0 else 1
    corner = s > 1 and t >= 2 * pair
    stars = mass.shape[1]
    cap = idx.shape[0]
    ia, ja = lax.axis_index("ia"), lax.axis_index("ja")
    hi, lo = ja // n_lo, ja % n_lo
    me = lo * n_ia + ia
    mesh_id = pl.DeviceIdType.MESH

    home = (hi == 0) & (me < pair) & corner
    remote = (hi == s - 1) & (me >= t - pair) & corner
    between = (hi == 0) & (me >= t - pair) & corner

    chip = 2 if flip else 1

    def distance(p):
        return p // n_ia + (p % n_ia) // chip

    mine = distance(me)
    side = n_ia // chip
    nearer = sum(chip * jnp.clip(mine - k, 0, side) for k in range(n_lo)) + me % chip
    farther = sum(chip * (side - jnp.clip(mine - k + 1, 0, side)) for k in range(n_lo))
    farther = farther + chip - 1 - me % chip

    def beyond(p):
        return (distance(p) > mine) | ((p // chip == me // chip) & (p > me))

    def before(p):
        return (distance(p) < mine) | ((p // chip == me // chip) & (p < me))

    def mate(p):
        return (p % n_ia, hi * n_lo + p // n_ia)

    def partner(o):
        other = ia + 1 - 2 * (ia % 2) if flip else ia
        return (other, o * n_lo + lo)

    def nearest(o):
        up = o + jnp.where(o >= hi, 1, 0)
        down = s - 1 - o - jnp.where(o >= s - 1 - hi, 1, 0)
        return jnp.where(2 * hi < s, up, down)

    def src_copy(o):
        return pltpu.make_async_remote_copy(
            src_ref=src.at[hi], dst_ref=src.at[hi], send_sem=src_send,
            recv_sem=src_recv.at[hi - jnp.where(hi > o, 1, 0)], device_id=partner(o), device_id_type=mesh_id)

    def corner_of():
        p = t - 1 - me
        return (p % n_ia, jnp.where(hi == 0, s - 1, 0) * n_lo + p // n_ia)

    def corner_copy():
        return pltpu.make_async_remote_copy(
            src_ref=src.at[hi], dst_ref=src.at[s], send_sem=src_send,
            recv_sem=src_recv.at[s - 1], device_id=corner_of(), device_id_type=mesh_id)

    def tgt_copy(p):
        return pltpu.make_async_remote_copy(
            src_ref=tgt.at[me], dst_ref=tgt.at[me], send_sem=tgt_send,
            recv_sem=tgt_recv.at[jnp.where(p // pair == me // pair, 2, jnp.where(me < pair, 0, 1))],
            device_id=mate(p),
            device_id_type=mesh_id)

    def red_copy(p):
        return pltpu.make_async_remote_copy(
            src_ref=part.at[p], dst_ref=got.at[me], send_sem=red_send,
            recv_sem=red_recv, device_id=mate(p), device_id_type=mesh_id)

    def wait_for(ref, n, sem):
        if n > 0:
            pltpu.make_async_copy(ref.at[0:n], ref.at[0:n], sem).wait()

    def each(low, high, body):
        def step(k, carry):
            body(k)
            return carry
        lax.fori_loop(low, high, step, 0)

    def others(body):
        def step(p):
            @pl.when(p != me)
            def other():
                body(p)

        if t > UNROLLED:
            each(0, t, step)
        else:
            for p in range(t):
                step(p)

    barrier = pltpu.get_barrier_semaphore()

    def signal(semaphore, device):
        pl.semaphore_signal(semaphore, inc=1, device_id=device, device_id_type=mesh_id)

    loads = [
        pltpu.make_async_copy(a, b, in_sem.at[i])
        for i, a, b in [
            (0, pos_hbm, big.at[0]), (0, vel_hbm, big.at[1]), (0, acc_hbm, big.at[2]),
            (0, jerk_hbm, big.at[3]), (1, level_hbm, level), (2, mass_hbm, mass),
            (3, idx_hbm, idx)]
    ]
    @pl.when(hi == 0)
    def greet_all():
        others(lambda p: signal(barrier, mate(p)))

    for load in loads:
        load.start()

    each(hi + 1, s, lambda o: signal(barrier, partner(o)))

    @pl.when(home)
    def greet_corner():
        signal(barrier, corner_of())

    def greet(p):
        @pl.when((hi > 0) & beyond(p))
        def hello():
            signal(barrier, mate(p))

    others(greet)

    @pl.when(hi > 0)
    def near_here():
        pl.semaphore_wait(barrier, hi + nearer + jnp.where(remote, 1, 0))
        each(0, hi, lambda o: signal(ready.at[hi - 1], partner(o)))

    wait_for(big, 4, in_sem.at[0])
    loads[4].wait()
    loads[5].wait()

    pos, vel, acc, jerk = [big[i] for i in range(4)]
    periods = jnp.left_shift(jnp.ones((1, stars), jnp.int32), top_level - level[...])
    remains = jnp.bitwise_and(tick_now, periods - 1)
    age = jnp.where(remains == 0, periods, remains).astype(jnp.float32) * tick_length
    src[hi, 0:3] = pos + age * (vel + age * (acc * 0.5 + age * jerk * (1.0 / 6.0)))
    src[hi, 3:6] = vel + age * (acc + age * jerk * 0.5)
    src[hi, 6:7] = mass[...]

    @pl.when(remote)
    def to_home():
        corner_copy().start()

    @pl.when(hi > 0)
    def to_first_part():
        src_copy(0).start()

    @pl.when(hi > 0)
    def answer():
        def tell(p):
            @pl.when(before(p))
            def back():
                signal(mates, mate(p))

        others(tell)


    loads[6].wait()
    slot = lax.broadcasted_iota(jnp.int32, (cap, stars), 0)
    want = jnp.zeros((cap, stars), jnp.int32)
    for i in range(cap):
        want = jnp.where(slot == i, idx[i], want)
    mask = lax.broadcasted_iota(jnp.int32, (cap, stars), 1) == want

    def pick(row):
        return jnp.sum(jnp.where(mask, row, 0.0), axis=1, keepdims=True)

    lane = lax.broadcasted_iota(jnp.int32, (cap, LANES), 1)

    def columns(values):
        tile = jnp.zeros((cap, LANES), jnp.float32)
        for i, value in values:
            tile = jnp.where(lane == i, value, tile)
        return tile

    own = [pick(src[hi, q:q + 1]) for q in range(6)]
    tgt[me] = columns(enumerate(own))

    each(1, hi, lambda o: src_copy(o).start())

    early = jnp.where((hi > 0) & (mine == 0), s, hi + 1)

    def reply(o):
        pl.semaphore_wait(ready.at[o - 1], 1)
        src_copy(o).start()

    each(hi + 1, early, reply)

    @pl.when(hi == 0)
    def all_here():
        pl.semaphore_wait(barrier, t - 1)

    @pl.when((hi > 0) & (farther > 0))
    def far_here():
        pl.semaphore_wait(mates, farther)

    others(lambda p: tgt_copy(p).start())

    old_acc = [pick(big[2, q:q + 1, :]) for q in range(3)]
    old_jerk = [pick(big[3, q:q + 1, :]) for q in range(3)]
    h = pick(age)
    live = pick(level[...].astype(jnp.float32)) > first_active_level - 0.5
    h2 = h * h
    fixed = [own[q] - h2 * (0.15 * old_acc[q] + (7.0 / 60.0) * h * old_jerk[q])
             for q in range(3)]
    fixed += [own[3 + q] - h * (0.5 * old_acc[q] + (5.0 / 12.0) * h * old_jerk[q])
              for q in range(3)]
    constant = columns(enumerate(fixed))
    factor = columns([(q, 0.15 * h2) for q in range(3)] + [(3 + q, 0.5 * h) for q in range(3)]
                     + [(6 + q, 1.0) for q in range(6)]
                     + [(FAR + q, h2 * h * (-1.0 / 30.0)) for q in range(3)]
                     + [(FAR + 3 + q, h2 * (-1.0 / 12.0)) for q in range(3)])

    kind = jnp.full((cap, LANES), -1, jnp.int32)
    for i in range(9):
        kind = jnp.where(lane == i, i % 3, kind)
    for q in range(3):
        kind = jnp.where(lane == 9 + q, 3 + q, kind)
    for i in range(6):
        kind = jnp.where(lane == FAR + i, 3 + i % 3, kind)

    def late(i):
        reply(jnp.where((hi == 0) & (i > 1) & (me % chip == 0), s + 1 - i, i))

    each(early, s, late)

    def pairs(targets, j, totals):
        totals = [list(total) for total in totals]
        for c in range(stars // LANES):
            row = [src[j, q:q + 1, c * LANES:(c + 1) * LANES] for q in range(7)]
            for target, total in zip(targets, totals):
                d = [row[q] - target[q] for q in range(3)]
                w = [row[3 + q] - target[3 + q] for q in range(3)]
                u = lax.rsqrt(d[0] * d[0] + d[1] * d[1] + d[2] * d[2] + soft_square)
                u2 = u * u
                m = row[6] * u * u2
                r = 3.0 * (d[0] * w[0] + d[1] * w[1] + d[2] * w[2]) * u2
                for q in range(3):
                    total[q] = total[q] + m * d[q]
                    total[3 + q] = total[3 + q] + m * (w[q] - r * d[q])
        return totals

    def spread(k):
        tile = tgt[k]
        return [jnp.broadcast_to(tile[:, q:q + 1], (cap, LANES)) for q in range(6)]

    def zeros():
        return [[jnp.zeros((cap, LANES), jnp.float32)] * 6 for _ in range(pair)]

    def widen(i):
        for k in [i * pair + b for b in range(pair)]:
            for q, value in enumerate(spread(k)):
                wide[k, q] = value

    def first(i, fresh=True):
        ks = [i * pair + b for b in range(pair)]
        if fresh:
            targets = [spread(k) for k in ks]
            for k, target in zip(ks, targets):
                for q in range(6):
                    wide[k, q] = target[q]
        else:
            targets = [[wide[k, q] for q in range(6)] for k in ks]
        for k, total in zip(ks, pairs(targets, hi, zeros())):
            for q in range(6):
                sums[k, q] = total[q]

    def held(i):
        ks = [i * pair + b for b in range(pair)]
        return [[sums[k, q] for q in range(6)] for k in ks]

    def added(i, j):
        ks = [i * pair + b for b in range(pair)]
        return pairs([[wide[k, q] for q in range(6)] for k in ks], j, held(i))

    def add(i, j):
        for b, total in enumerate(added(i, j)):
            for q in range(6):
                sums[i * pair + b, q] = total[q]

    def finish(i, totals):
        ks = [i * pair + b for b in range(pair)]
        forces = [[jnp.sum(x, axis=1, keepdims=True) for x in total] for total in totals]
        for k, force in zip(ks, forces):
            tile = jnp.zeros((cap, LANES), jnp.float32)
            for q in range(6):
                tile = jnp.where(kind == q, force[q], tile)
            part[k] = tile
        for k in ks:
            @pl.when(k != me)
            def send(k=k):
                red_copy(k).start()

    def arrival(j):
        pltpu.make_async_copy(
            src.at[j], src.at[j], src_recv.at[j - jnp.where(j > hi, 1, 0)]).wait()

    ours = me // pair
    wait_for(tgt, pair - 1, tgt_recv.at[2])
    first(ours)

    few = t <= UNROLLED

    def first_of_others(i):
        @pl.when(i != ours)
        def other_pair():
            first(i, not few)

    turn = jnp.where((hi > 0) & (mine > 0) & (mine < n_lo + n_ia // chip - 2), 0, 1)

    def take(k):
        @pl.when((k == turn) & (ours > 0))
        def first_pair():
            wait_for(tgt, pair, tgt_recv.at[0])
            first(0)

        @pl.when(k != turn)
        def other_pairs():
            @pl.when(ours == 0)
            def near():
                wait_for(tgt, t - pair, tgt_recv.at[1])

            @pl.when(ours > 0)
            def far():
                wait_for(tgt, t - 2 * pair, tgt_recv.at[1])

            if few:
                for i in range(1, t // pair):
                    widen(i)
            each(1, t // pair, first_of_others)

    each(0, 2, take)

    def near_block(o):
        j = nearest(o)
        arrival(j)
        add(0, j)

    each(0, s - 2, near_block)
    end = nearest(s - 2) if s > 1 else hi

    if s > 1:
        @pl.when(jnp.logical_not(between))
        def last_block():
            arrival(end)
            add(0, end)

    @pl.when(jnp.logical_not(home))
    def first_pair():
        finish(0, held(0))

    each(1, t // pair, lambda i: each(0, s - 2, lambda o: add(i, nearest(o))))
    if corner:
        @pl.when(between)
        def last_arrival():
            arrival(end)

    each(1, t // pair, lambda i: finish(i, added(i, end) if s > 1 else held(i)))

    if corner:
        @pl.when(home)
        def corner_block():
            arrival(s)
            finish(0, added(0, s))

    got[me] = part[me]

    wait_for(got, t - 1, red_recv)
    if t > UNROLLED:
        total = lax.fori_loop(0, t, lambda p, total: total + got[p],
                              jnp.zeros((cap, LANES), jnp.float32)) * factor
    else:
        tiles = [got[p] for p in range(t)]
        while len(tiles) > 1:
            tiles = [sum(tiles[i:i + 2]) for i in range(0, len(tiles), 2)]
        total = tiles[0] * factor
    result = constant + total + pltpu.roll(total, LANES - FAR, 1)
    out_ref[...] = jnp.where(live, result, 0.0)[:, :12]

    wait_for(part, t - 1, red_send)
    wait_for(tgt, t - 1, tgt_send)

    @pl.when(remote)
    def sent_corner():
        wait_for(src, s, src_send)

    @pl.when(jnp.logical_not(remote))
    def sent():
        wait_for(src, s - 1, src_send)


def on_device(shape, star_pos, star_vel, star_acc, star_jerk, star_mass, star_level,
              active_index, active_count):
    del active_count
    n_ia, n_ja, s = shape
    t = n_ia * (n_ja // s)
    stars = star_mass.shape[0]
    cap = active_index.shape[0]
    f32 = jnp.float32
    return pl.pallas_call(
        functools.partial(kernel, shape),
        out_shape=pltpu.VMEM((cap, 12), f32),
        in_specs=[pl.BlockSpec(memory_space=pltpu.HBM)] * 7,
        out_specs=pl.BlockSpec(memory_space=pltpu.VMEM),
        scratch_shapes=[
            pltpu.VMEM((4, 3, stars), f32),
            pltpu.VMEM((1, stars), f32), pltpu.VMEM((1, stars), jnp.int32),
            pltpu.SMEM((cap,), jnp.int32),
            pltpu.VMEM((s + 1, 7, stars), f32),
            pltpu.VMEM((t, cap, LANES), f32),
            pltpu.VMEM((t, 6, cap, LANES), f32),
            pltpu.VMEM((t, 6, cap, LANES), f32),
            pltpu.VMEM((t, cap, LANES), f32),
            pltpu.VMEM((t, cap, LANES), f32),
            pltpu.SemaphoreType.DMA((4,)),
            pltpu.SemaphoreType.DMA, pltpu.SemaphoreType.DMA((s,)),
            pltpu.SemaphoreType.DMA, pltpu.SemaphoreType.DMA((3,)),
            pltpu.SemaphoreType.DMA, pltpu.SemaphoreType.DMA,
            pltpu.SemaphoreType.REGULAR((max(s - 1, 1),)), pltpu.SemaphoreType.REGULAR,
        ],
        compiler_params=pltpu.CompilerParams(collective_id=0, has_side_effects=True),
    )(star_pos, star_vel, star_acc, star_jerk, star_mass.reshape(1, stars),
      star_level.reshape(1, stars), active_index).T


def solution(mesh):
    n_ia, n_ja = mesh.shape["ia"], mesh.shape["ja"]
    s = SOURCE_PARTS if n_ja % SOURCE_PARTS == 0 else 1
    columns = P(None, ("ia", "ja"))
    flat = P(("ia", "ja"))
    return jax.shard_map(
        functools.partial(on_device, (n_ia, n_ja, s)), mesh=mesh,
        in_specs=(columns,) * 4 + (flat,) * 4, out_specs=columns, check_vma=False)
```
